256 devices in a mesh: section: 4 (over x), dp: 64 (over z, y, core).
Axes of the slice: x: 4, y: 4, z: 8, core: 2. Of those that a mesh axis runs over, the one named last changes fastest.
Arguments:
- out_grad: bfloat16 [8192, 5120], P('dp', 'section'), may hold values from -0.26367188 to 0.26367188
- pre_act: bfloat16 [4, 8192, 27648], P('section', 'dp'), may hold values from -6 to 6
- down_a: bfloat16 [4, 27648, 32], P('section'), may hold values from -1 to 1
- down_b: bfloat16 [4, 32, 5120], P('section'), may hold values from -0.078125 to 0.078125
- up_a: bfloat16 [4, 5120, 32], P('section'), may hold values from -1 to 1
- up_b: bfloat16 [4, 27648, 32], P('section'), may hold values from -0.0390625 to 0.0390625
- master: float32 [4, 4, 6912, 32], P('section', None, 'dp'), may hold values from -1 to 1
- moment: float32 [4, 4, 6912, 32], P('section', None, 'dp'), may hold values from -3 to 3
- second: float32 [4, 4, 6912, 32], P('section', None, 'dp'), may hold values from 0.2 to 4
Outputs:
- new_weight: bfloat16 [4, 27648, 32], P('section')
- new_master: float32 [4, 4, 6912, 32], P('section', None, 'dp')
- new_moment: float32 [4, 4, 6912, 32], P('section', None, 'dp')
- new_second: float32 [4, 4, 6912, 32], P('section', None, 'dp')
The draws below stay inside these ranges and needn't reach their ends.
All inputs are finite; a program needn't handle non-finite values.
Results may differ from the reference program's by a relative error of at most 0.014.
Values may be sent and summed in bfloat16 or wider, within the bound.
No kernel may reach another device: no remote copies, remote signals or barrier semaphores. Data moves between devices by JAX's collectives and lax.ppermute only.
A program may use at most 128 MiB of HBM per device.

```python
import math
import jax
import jax.numpy as jnp

D = 5120
FF = 27648
R = 32
BUCKETS = 4
STEP = 20
SECTIONS = 4
BUCKET_ROWS = 6912
TOKENS = 8192


def steps_of(key, extent, shards, least, top_value):
    factor_of = 1.0
    for dim, parts in shards:
        heights = jax.random.uniform(jax.random.fold_in(jax.random.fold_in(key, 6), dim), (parts,), jnp.float32, least / len(shards), top_value / len(shards))
        factor_of = factor_of * jnp.repeat(jnp.exp(heights), extent[dim] // parts).reshape((-1,) + (1,) * (len(extent) - 1 - dim))
    return factor_of


def noise(key, shape, spread, most, pieces=(), dtype=jnp.bfloat16):
    entries = jax.random.normal(key, shape, jnp.float32) * spread
    if len(pieces) > 0:
        entries = steps_of(key, shape, pieces, -0.22, 0.18) * entries
    return jnp.clip(entries, min=-most, max=most).astype(dtype)


def setup_inputs(seed: int = 0) -> dict:
    splits = jax.random.split(jax.random.key(seed), 10)
    return {
        "out_grad": noise(splits[0], (TOKENS, D), (4 * TOKENS ** -0.5), 0.26367188, ((0, 64), (1, 4))),
        "pre_act": noise(splits[1], (SECTIONS, TOKENS, FF), 1.5, 6.0, ((0, 4), (1, 64))),
        "down_a": noise(splits[2], (SECTIONS, FF, R), R ** -0.5, 1.0, ((0, 4),)),
        "down_b": noise(splits[3], (SECTIONS, R, D), D ** -0.5, 0.078125, ((0, 4),)),
        "up_a": noise(splits[4], (SECTIONS, D, R), R ** -0.5, 1.0, ((0, 4),)),
        "up_b": noise(splits[5], (SECTIONS, FF, R), FF ** -0.5, 0.0390625, ((0, 4),)),
        "master": noise(splits[6], (SECTIONS, BUCKETS, BUCKET_ROWS, R), R ** -0.5, 1.0, ((0, 4), (2, 64)), jnp.float32),
        "moment": noise(splits[7], (SECTIONS, BUCKETS, BUCKET_ROWS, R), 0.5, 3.0, ((0, 4), (2, 64)), jnp.float32),
        "second": jnp.clip(jnp.exp(math.log(4.0) - 2.9957323 * jax.random.uniform(splits[8], (SECTIONS, BUCKETS, BUCKET_ROWS, R), jnp.float32) ** steps_of(splits[8], (SECTIONS, BUCKETS, BUCKET_ROWS, R), ((0, 4), (2, 64)), -0.2, 0.2)), 0.2, 4.0),
    }


BETA_ONE = 0.8
BETA_TWO = 0.95
LEARN_RATE = 0.02
DECAY_RATE = 0.1
EPSILON = 1e-08

def slope_of(values):
    sigm = jax.nn.sigmoid(values)
    return sigm * (1.0 + values * (1.0 - sigm))

def adamw(gradient, weights, first, seconds):
    first_new = BETA_ONE * first + (1.0 - BETA_ONE) * gradient
    second_new = BETA_TWO * seconds + (1.0 - BETA_TWO) * gradient * gradient
    first_hat = first_new / (1.0 - BETA_ONE ** STEP)
    second_hat = second_new / (1.0 - BETA_TWO ** STEP)
    weights_new = weights - LEARN_RATE * (first_hat / (jnp.sqrt(second_hat) + EPSILON) + DECAY_RATE * weights)
    return (weights_new, first_new, second_new)

def reference(out_grad, pre_act, down_a, down_b, up_a, up_b, master, moment, second):
    incoming = out_grad
    weights_out = [None] * SECTIONS
    masters_out = [None] * SECTIONS
    moments_out = [None] * SECTIONS
    seconds_out = [None] * SECTIONS
    for section_pos in reversed(range(SECTIONS)):
        inputs = pre_act[section_pos].astype(jnp.float32)
        hidden = jax.nn.silu(inputs).astype(jnp.bfloat16)
        low = jnp.dot(incoming, down_b[section_pos].T, preferred_element_type=jnp.float32).astype(jnp.bfloat16)
        gradient = jnp.dot(hidden.T, low, preferred_element_type=jnp.float32)
        if section_pos > 0:
            upstream = jnp.dot(low, down_a[section_pos].T, preferred_element_type=jnp.float32)
            delta = (upstream * slope_of(inputs)).astype(jnp.bfloat16)
            back_low = jnp.dot(delta, up_b[section_pos], preferred_element_type=jnp.float32).astype(jnp.bfloat16)
            carried = jnp.dot(back_low, up_a[section_pos].T, preferred_element_type=jnp.float32)
            incoming_next = (incoming.astype(jnp.float32) + carried).astype(jnp.bfloat16)
        gradient = gradient.reshape(BUCKETS, BUCKET_ROWS, R)
        weights_new, first_new, second_new = adamw(gradient, master[section_pos], moment[section_pos], second[section_pos])
        masters_out[section_pos] = weights_new
        moments_out[section_pos] = first_new
        seconds_out[section_pos] = second_new
        weights_out[section_pos] = weights_new.astype(jnp.bfloat16).reshape(FF, R)
        if section_pos > 0:
            incoming = incoming_next
    return (jnp.stack(weights_out), jnp.stack(masters_out), jnp.stack(moments_out), jnp.stack(seconds_out))
```

```python
import functools

import jax
import jax.numpy as jnp
from jax import lax
from jax.experimental import pallas as pl
from jax.experimental.pallas import tpu as pltpu
from jax.sharding import PartitionSpec as P

BUCKETS = 4
STEP = 20
BETA_ONE = 0.8
BETA_TWO = 0.95
LEARN_RATE = 0.02
DECAY_RATE = 0.1
EPSILON = 1e-08

TOKENS = 128
FF = 27648
RANK = 32
MODEL = 5120
WIDTH = MODEL // 4
BUCKET_ROWS = FF // BUCKETS
OWNED = 108
LANES = 128
ZS, YS = 8, 4
BF16, F32 = jnp.bfloat16, jnp.float32
VMEM = pl.BlockSpec(memory_space=pltpu.VMEM)
CONTRACT_LAST = (((1,), (1,)), ((), ()))


def params(mib=48):
    return pltpu.CompilerParams(vmem_limit_bytes=mib * 1024 * 1024)


def shaped(shape, dtype):
    return jax.ShapeDtypeStruct(shape, dtype)


def z_pos():
    return lax.axis_index("dp") // 8


def y_pos():
    return (lax.axis_index("dp") // 2) % YS


def core_pos():
    return lax.axis_index("dp") % 2


def over_dp(value, dz=0, dy=0, dc=0):
    pairs = []
    for z in range(ZS):
        for y in range(YS):
            for c in range(2):
                target = ((z + dz) % ZS) * 8 + ((y + dy) % YS) * 2 + (c + dc) % 2
                pairs.append((z * 8 + y * 2 + c, target))
    return lax.ppermute(value, "dp", pairs)


def over_section(value, steps):
    return lax.ppermute(value, "section", [(i, (i + steps) % 4) for i in range(4)])


def slice_kernel(db_ref, ua_ref, *outs):
    here = lax.axis_index("section")
    for k, out in enumerate(outs):
        columns = pl.ds(pl.multiple_of(lax.rem(here + k, 4) * WIDTH, LANES), WIDTH)
        out[0:RANK, :] = db_ref[:, columns]
        out[RANK:, :] = ua_ref[:, columns]


def slices(db, ua):
    return pl.pallas_call(
        slice_kernel,
        out_shape=[shaped((2 * RANK, WIDTH), BF16)] * 4,
        in_specs=[VMEM] * 2,
        out_specs=[VMEM] * 4,
        name="slices",
    )(db, ua)


def prep_kernel(pre_ref, hidden_ref, slope_ref):
    v = pre_ref[...].astype(F32)
    s = 0.5 + 0.5 * jnp.tanh(0.5 * v)
    h = v * s
    hidden_ref[...] = h.astype(BF16)
    slope_ref[...] = (s + h * (1.0 - s)).astype(BF16)


def prep(pre):
    block = pl.BlockSpec((TOKENS, 3072), lambda i: (0, i))
    return pl.pallas_call(
        prep_kernel,
        grid=(FF // 3072,),
        out_shape=[shaped((TOKENS, FF), BF16)] * 2,
        in_specs=[block],
        out_specs=[block] * 2,
        compiler_params=params(),
        cost_estimate=pl.CostEstimate(
            flops=10 * TOKENS * FF, bytes_accessed=6 * TOKENS * FF, transcendentals=TOKENS * FF
        ),
        name="prep",
    )(pre)


def share_kernel(g_ref, w0, w1, w2, w3, *outs):
    ws = (w0, w1, w2, w3)
    for k, out in enumerate(outs):
        db = ws[k][0:RANK, :]
        out[:, 0:LANES] = lax.dot_general(
            db, g_ref[...], CONTRACT_LAST, preferred_element_type=F32
        )
        rows = jnp.concatenate([ws[(k - m) % 4][RANK:, :] for m in (1, 2, 3, 0)], axis=0)
        out[:, LANES:] = lax.dot_general(db, rows, CONTRACT_LAST, preferred_element_type=F32)


def shares(g, ws):
    return pl.pallas_call(
        share_kernel,
        out_shape=[shaped((RANK, 2 * LANES), F32)] * 4,
        in_specs=[VMEM] * 5,
        out_specs=[VMEM] * 4,
        compiler_params=params(),
        name="shares",
    )(g, *ws)


def low_of(share_refs, above_ref):
    total = share_refs[0][...] + share_refs[1][...] + share_refs[2][...] + share_refs[3][...]
    low = total[:, 0:LANES]
    if above_ref is not None:
        low = low + jnp.dot(
            total[:, LANES : LANES + 3 * RANK],
            above_ref[...].astype(F32),
            preferred_element_type=F32,
            precision=lax.Precision.HIGHEST,
        )
    return low


RELAY_COLUMNS = 4608


def relay_kernel(first, *refs):
    share_refs, refs = refs[:4], refs[4:]
    above_ref = None
    if not first:
        above_ref, refs = refs[0], refs[1:]
    slope_ref, da_ref, ub_ref, out_ref, low, total = refs
    step = pl.program_id(0)

    @pl.when(step == 0)
    def _():
        low[...] = low_of(share_refs, above_ref).T.astype(BF16)
        total[...] = jnp.zeros_like(total)

    upstream = jnp.dot(low[...], da_ref[...], preferred_element_type=F32)
    delta = (upstream * slope_ref[...].astype(F32)).astype(BF16)
    total[...] += lax.dot_general(
        ub_ref[...], delta, CONTRACT_LAST, preferred_element_type=F32
    )

    @pl.when(step == pl.num_programs(0) - 1)
    def _():
        out_ref[0:RANK, :] = total[...].astype(BF16)
        if first:
            out_ref[RANK:, :] = jnp.zeros((2 * RANK, LANES), BF16)
        else:
            out_ref[RANK:, :] = above_ref[0 : 2 * RANK, :]


def relay(share, above, slope, da, ub):
    whole = pl.BlockSpec((RANK, 2 * LANES), lambda i: (0, 0))
    message = pl.BlockSpec((3 * RANK, LANES), lambda i: (0, 0))
    rank_block = pl.BlockSpec((RANK, RELAY_COLUMNS), lambda i: (0, i))
    first = above is None
    return pl.pallas_call(
        functools.partial(relay_kernel, first),
        grid=(FF // RELAY_COLUMNS,),
        out_shape=shaped((3 * RANK, LANES), BF16),
        in_specs=[whole] * 4
        + ([] if first else [message])
        + [pl.BlockSpec((TOKENS, RELAY_COLUMNS), lambda i: (0, i)), rank_block, rank_block],
        out_specs=message,
        scratch_shapes=[pltpu.VMEM((TOKENS, RANK), BF16), pltpu.VMEM((RANK, TOKENS), F32)],
        compiler_params=params(),
        name="relay_first" if first else "relay",
    )(*share, *([] if first else [above]), slope, da, ub)


def grad_kernel(s0, s1, s2, s3, above_ref, hidden_ref, keep_ref, send_ref, low, grad):
    @pl.when(pl.program_id(0) == 0)
    def _():
        low[...] = low_of((s0, s1, s2, s3), above_ref).astype(BF16)

    grad[...] = jnp.dot(low[...], hidden_ref[...], preferred_element_type=F32)
    core = core_pos()
    lane = lax.broadcasted_iota(jnp.int32, (RANK, LANES), 1)
    for z in range(ZS):
        for y in range(YS):
            pair = []
            for c in range(2):
                start = (z * 8 + y * 2 + c) * OWNED
                base, shift = start // LANES * LANES, start % LANES
                piece = grad[:, base : base + LANES]
                if shift:
                    piece = pltpu.roll(piece, LANES - shift, 1)
                if shift + OWNED > LANES:
                    more = pltpu.roll(
                        grad[:, base + LANES : base + 2 * LANES], LANES - shift, 1
                    )
                    piece = jnp.where(lane < LANES - shift, piece, more)
                pair.append(piece)
            keep_ref[y, z, 0] = jnp.where(core == 0, pair[0], pair[1]).astype(BF16)
            send_ref[y, z, 0] = jnp.where(core == 0, pair[1], pair[0]).astype(BF16)


def grads(share, above, hidden):
    whole = pl.BlockSpec((RANK, 2 * LANES), lambda i: (0, 0))
    half = pl.BlockSpec((YS, ZS, 1, RANK, LANES), lambda i: (0, 0, i, 0, 0))
    return pl.pallas_call(
        grad_kernel,
        grid=(BUCKETS,),
        out_shape=[shaped((YS, ZS, BUCKETS, RANK, LANES), BF16)] * 2,
        in_specs=[whole] * 4
        + [
            pl.BlockSpec((3 * RANK, LANES), lambda i: (0, 0)),
            pl.BlockSpec((TOKENS, BUCKET_ROWS), lambda i: (0, i)),
        ],
        out_specs=[half] * 2,
        scratch_shapes=[
            pltpu.VMEM((RANK, TOKENS), BF16),
            pltpu.VMEM((RANK, BUCKET_ROWS), F32),
        ],
        compiler_params=params(),
        name="grads",
    )(*share, above, hidden)


def core_sum_kernel(keep_ref, got_ref, own_ref, *outs):
    here = y_pos()
    own_ref[...] = keep_ref[here].astype(F32) + got_ref[here].astype(F32)
    for k, out in enumerate(outs):
        there = lax.rem(here + k + 1, YS)
        out[...] = (keep_ref[there].astype(F32) + got_ref[there].astype(F32)).astype(BF16)


def core_sum(keep, got):
    block = (ZS, BUCKETS, RANK, LANES)
    return pl.pallas_call(
        core_sum_kernel,
        out_shape=[shaped(block, F32)] + [shaped(block, BF16)] * 3,
        in_specs=[VMEM] * 2,
        out_specs=[VMEM] * 4,
        compiler_params=params(),
        name="core_sum",
    )(keep, got)


def y_sum_kernel(own_ref, g1, g2, g3, out_own, *outs):
    here = z_pos()

    def total(z):
        return own_ref[z] + g1[z].astype(F32) + g2[z].astype(F32) + g3[z].astype(F32)

    out_own[...] = total(here)
    for k, out in enumerate(outs):
        out[...] = total(lax.rem(here + k + 1, ZS)).astype(BF16)


def y_sum(own, got):
    block = (BUCKETS, RANK, LANES)
    return pl.pallas_call(
        y_sum_kernel,
        out_shape=[shaped(block, F32)] + [shaped(block, BF16)] * 7,
        in_specs=[VMEM] * 4,
        out_specs=[VMEM] * 8,
        compiler_params=params(),
        name="y_sum",
    )(own, *got)


def adamw_kernel(own_ref, g1, g2, g3, g4, g5, g6, g7, master, moment, second, *outs):
    weight_out, master_out, moment_out, second_out = outs
    gradient = own_ref[...]
    for got in (g1, g2, g3, g4, g5, g6, g7):
        gradient = gradient + got[...].astype(F32)
    gradient = gradient[:, :, 0:OWNED]
    weights = master[...]
    first_new = BETA_ONE * moment[...] + (1.0 - BETA_ONE) * gradient
    second_new = BETA_TWO * second[...] + (1.0 - BETA_TWO) * gradient * gradient
    first_hat = first_new / (1.0 - BETA_ONE**STEP)
    second_hat = second_new / (1.0 - BETA_TWO**STEP)
    weights_new = weights - LEARN_RATE * (
        first_hat / (jnp.sqrt(second_hat) + EPSILON) + DECAY_RATE * weights
    )
    weight_out[...] = jnp.zeros_like(weight_out)
    weight_out[:, :, 0:OWNED] = weights_new.astype(BF16)
    master_out[...] = weights_new
    moment_out[...] = first_new
    second_out[...] = second_new


def adamw(own, got, master, moment, second):
    state = shaped((BUCKETS, RANK, OWNED), F32)
    return pl.pallas_call(
        adamw_kernel,
        out_shape=[shaped((BUCKETS, RANK, LANES), BF16)] + [state] * 3,
        in_specs=[VMEM] * 11,
        out_specs=[VMEM] * 4,
        compiler_params=params(),
        name="adamw",
    )(own, *got, master, moment, second)


def assemble_kernel(*refs):
    arrays, (out_ref, blocks, sems) = refs[:8], refs[8:]
    core, y_here, z_here = core_pos(), y_pos(), z_pos()
    copies = []
    for side in range(2):
        for k in range(YS):
            copies.append(
                pltpu.make_async_copy(
                    arrays[side * YS + k],
                    blocks.at[lax.rem(core + side, 2), lax.rem(y_here + YS - k, YS)],
                    sems.at[side * YS + k],
                )
            )
            copies[-1].start()
    for copy in copies:
        copy.wait()
    lane = lax.broadcasted_iota(jnp.int32, (RANK, LANES), 1)
    for tile in range(FF // LANES):
        value = None
        first = tile * LANES // OWNED
        last = (tile * LANES + LANES - 1) // OWNED
        for piece in range(first, last + 1):
            bucket, owner = divmod(piece, 64)
            z, y, c = owner // 8, owner // 2 % YS, owner % 2
            block = blocks[c, y, lax.rem(z_here + ZS - z, ZS), bucket].astype(F32)
            start = piece * OWNED - tile * LANES
            if start % LANES:
                block = pltpu.roll(block, start % LANES, 1)
            value = block if value is None else jnp.where(lane < start, value, block)
        out_ref[:, tile * LANES : (tile + 1) * LANES] = value.astype(BF16)


def assemble(arrays):
    return pl.pallas_call(
        assemble_kernel,
        out_shape=shaped((RANK, FF), BF16),
        in_specs=[pl.BlockSpec(memory_space=pl.ANY)] * 8,
        out_specs=VMEM,
        scratch_shapes=[
            pltpu.VMEM((2, YS, ZS, BUCKETS, RANK, LANES), BF16),
            pltpu.SemaphoreType.DMA((8,)),
        ],
        compiler_params=params(),
        name="assemble",
    )(*arrays)


def per_device(out_grad, pre_act, down_a, down_b, up_a, up_b, master, moment, second):
    da, ub = down_a[0].T, up_b[0].T
    mine = slices(down_b[0], up_a[0].T)
    ws = [mine[0]] + [over_section(mine[k], k) for k in (1, 2, 3)]
    hidden, slope = prep(pre_act[0])
    share = shares(out_grad, ws)
    share = [share[0]] + [over_section(share[k], -k) for k in (1, 2, 3)]
    above = None
    for _ in range(3):
        sent = relay(share, above, slope, da, ub)
        above = lax.ppermute(sent, "section", [(1, 0), (2, 1), (3, 2)])
    keep, send = grads(share, above, hidden)
    own, *sends = core_sum(keep, over_dp(send, dc=1))
    own, *sends = y_sum(own, [over_dp(sends[k - 1], dy=k) for k in (1, 2, 3)])
    got = [over_dp(sends[k - 1], dz=k) for k in range(1, 8)]
    state = [a[0].transpose(0, 2, 1) for a in (master, moment, second)]
    weight, *state = adamw(own, got, *state)
    column = jnp.stack([weight] + [over_dp(weight, dz=k) for k in range(1, 8)])
    plane = [column] + [over_dp(column, dy=k) for k in (1, 2, 3)]
    rows = assemble(plane + [over_dp(a, dc=1) for a in plane])
    return (rows.T[None], *[a.transpose(0, 2, 1)[None] for a in state])


def solution(mesh):
    return jax.shard_map(
        per_device,
        mesh=mesh,
        in_specs=(
            P("dp", "section"),
            P("section", "dp", None),
            P("section", None, None),
            P("section", None, None),
            P("section", None, None),
            P("section", None, None),
            P("section", None, "dp", None),
            P("section", None, "dp", None),
            P("section", None, "dp", None),
        ),
        out_specs=(
            P("section", None, None),
            P("section", None, "dp", None),
            P("section", None, "dp", None),
            P("section", None, "dp", None),
        ),
        check_vma=False,
    )
```

```python
import functools

import jax
import jax.numpy as jnp
from jax import lax
from jax.experimental import pallas as pl
from jax.experimental.pallas import tpu as pltpu
from jax.sharding import PartitionSpec as P

BUCKETS = 4
STEP = 20
BETA_ONE = 0.8
BETA_TWO = 0.95
LEARN_RATE = 0.02
DECAY_RATE = 0.1
EPSILON = 1e-08

TOKENS = 128
FF = 27648
RANK = 32
MODEL = 5120
WIDTH = MODEL // 4
BUCKET_ROWS = FF // BUCKETS
OWNED = 108
LANES = 128
ZS, YS = 8, 4
BF16, F32 = jnp.bfloat16, jnp.float32
VMEM = pl.BlockSpec(memory_space=pltpu.VMEM)
ANY = pl.BlockSpec(memory_space=pl.ANY)
HBM = pl.BlockSpec(memory_space=pltpu.HBM)
CONTRACT_LAST = (((1,), (1,)), ((), ()))


def params(mib=16):
    return pltpu.CompilerParams(vmem_limit_bytes=mib * 1024 * 1024)


def shaped(shape, dtype):
    return jax.ShapeDtypeStruct(shape, dtype)


def z_pos():
    return lax.axis_index("dp") // 8


def y_pos():
    return (lax.axis_index("dp") // 2) % YS


def core_pos():
    return lax.axis_index("dp") % 2


def over_dp(value, zx=0, dy=0, dc=0):
    pairs = []
    for z in range(ZS):
        for y in range(YS):
            for c in range(2):
                target = (z ^ zx) * 8 + ((y + dy) % YS) * 2 + (c + dc) % 2
                pairs.append((z * 8 + y * 2 + c, target))
    return lax.ppermute(value, "dp", pairs)


def over_section(value, steps):
    return lax.ppermute(value, "section", [(i, (i + steps) % 4) for i in range(4)])


def slice_kernel(db_ref, ua_ref, *refs):
    outs, sems = refs[:4], refs[4]
    here = lax.axis_index("section")
    copies = []
    for k, out in enumerate(outs):
        columns = pl.ds(pl.multiple_of(lax.rem(here + k, 4) * WIDTH, LANES), WIDTH)
        for i, ref in enumerate((db_ref, ua_ref)):
            copies.append(
                pltpu.make_async_copy(
                    ref.at[:, columns], out.at[pl.ds(i * RANK, RANK), :], sems.at[2 * k + i]
                )
            )
            copies[-1].start()
    for copy in copies:
        copy.wait()


def slices(db, ua):
    return pl.pallas_call(
        slice_kernel,
        out_shape=[shaped((2 * RANK, WIDTH), BF16)] * 4,
        in_specs=[ANY] * 2,
        out_specs=[ANY] * 4,
        scratch_shapes=[pltpu.SemaphoreType.DMA((8,))],
        name="slices",
    )(db, ua)


def activation_kernel(slope, first, size, pre_ref, out_ref, held, sems):
    parts = held.shape[1] // size
    copies = []
    for i in range(parts):
        copies.append(
            pltpu.make_async_copy(
                pre_ref.at[:, pl.ds(first + i * size, size)],
                held.at[:, pl.ds(i * size, size)],
                sems.at[i],
            )
        )
        copies[-1].start()

    def chunk(i, _):
        columns = pl.ds(pl.multiple_of(i * 256, 256), 256)
        for row in range(0, TOKENS, 32):
            rows = slice(row, row + 32)
            half = 0.5 * held[rows, columns].astype(F32)
            t = jnp.tanh(half)
            h = half + half * t
            if slope:
                h = 0.5 * ((1.0 + t) + h * (1.0 - t))
            out_ref[rows, columns] = h.astype(BF16)
        return 0

    for i, copy in enumerate(copies):
        copy.wait()
        lax.fori_loop(i * size // 256, (i + 1) * size // 256, chunk, 0)


def activation(pre, bucket=None):
    slope = bucket is None
    width, first, size = (FF, 0, 6912) if slope else (BUCKET_ROWS, bucket * BUCKET_ROWS, 2304)
    parts = width // size
    return pl.pallas_call(
        functools.partial(activation_kernel, slope, first, size),
        out_shape=shaped((TOKENS, width), BF16),
        in_specs=[HBM],
        out_specs=VMEM,
        scratch_shapes=[
            pltpu.VMEM((TOKENS, width), BF16),
            pltpu.SemaphoreType.DMA((parts,)),
        ],
        compiler_params=params(18 if slope else 6),
        cost_estimate=pl.CostEstimate(
            flops=10 * TOKENS * width,
            bytes_accessed=4 * TOKENS * width,
            transcendentals=TOKENS * width,
        ),
        name="slope" if slope else "hidden",
    )(pre)


def share_kernel(g_ref, w0, w1, w2, w3, *outs):
    ws = (w0, w1, w2, w3)
    for k, out in enumerate(outs):
        db = ws[k][0:RANK, :]
        out[:, 0:LANES] = lax.dot_general(
            db, g_ref[...], CONTRACT_LAST, preferred_element_type=F32
        )
        rows = jnp.concatenate([ws[(k - m) % 4][RANK:, :] for m in (1, 2, 3, 0)], axis=0)
        out[:, LANES:] = lax.dot_general(db, rows, CONTRACT_LAST, preferred_element_type=F32)


def shares(g, ws):
    return pl.pallas_call(
        share_kernel,
        out_shape=[shaped((RANK, 2 * LANES), F32)] * 4,
        in_specs=[VMEM] * 5,
        out_specs=[VMEM] * 4,
        compiler_params=params(),
        name="shares",
    )(g, *ws)


def low_of(share_refs, above_ref):
    total = share_refs[0][...] + share_refs[1][...] + share_refs[2][...] + share_refs[3][...]
    low = total[:, 0:LANES]
    if above_ref is not None:
        low = low + jnp.dot(
            total[:, LANES : LANES + 3 * RANK],
            above_ref[...].astype(F32),
            preferred_element_type=F32,
            precision=lax.Precision.HIGHEST,
        )
    return low


def relay_kernel(first, *refs):
    share_refs, refs = refs[:4], refs[4:]
    above_ref = None
    if not first:
        above_ref, refs = refs[0], refs[1:]
    slope_ref, da_ref, ub_ref, out_ref = refs
    low = low_of(share_refs, above_ref).T.astype(BF16)

    def chunk(i, total):
        columns = pl.ds(pl.multiple_of(i * 512, 512), 512)
        upstream = jnp.dot(low, da_ref[:, columns], preferred_element_type=F32)
        delta = (upstream * slope_ref[:, columns].astype(F32)).astype(BF16)
        return total + lax.dot_general(
            ub_ref[:, columns], delta, CONTRACT_LAST, preferred_element_type=F32
        )

    total = lax.fori_loop(
        0, FF // 512, chunk, jnp.zeros((RANK, TOKENS), F32), unroll=18
    )
    out_ref[0:RANK, :] = total.astype(BF16)
    if first:
        out_ref[RANK:, :] = jnp.zeros((2 * RANK, LANES), BF16)
    else:
        out_ref[RANK:, :] = above_ref[0 : 2 * RANK, :]


def relay(share, above, slope, da, ub):
    first = above is None
    return pl.pallas_call(
        functools.partial(relay_kernel, first),
        out_shape=shaped((3 * RANK, LANES), BF16),
        in_specs=[VMEM] * (7 if first else 8),
        out_specs=VMEM,
        compiler_params=params(14),
        name="relay_first" if first else "relay",
    )(*share, *([] if first else [above]), slope, da, ub)


def grad_kernel(s0, s1, s2, s3, above_ref, h0, h1, h2, h3, keep_ref, send_ref, grad):
    low = low_of((s0, s1, s2, s3), above_ref).astype(BF16)
    core = core_pos()
    lane = lax.broadcasted_iota(jnp.int32, (RANK, LANES), 1)
    for bucket, hidden_ref in enumerate((h0, h1, h2, h3)):
        grad[...] = jnp.dot(low, hidden_ref[...], preferred_element_type=F32)
        for z in range(ZS):
            for y in range(YS):
                pair = []
                for c in range(2):
                    start = (z * 8 + y * 2 + c) * OWNED
                    base, shift = start // LANES * LANES, start % LANES
                    piece = grad[:, base : base + LANES]
                    if shift:
                        piece = pltpu.roll(piece, LANES - shift, 1)
                    if shift + OWNED > LANES:
                        more = pltpu.roll(
                            grad[:, base + LANES : base + 2 * LANES], LANES - shift, 1
                        )
                        piece = jnp.where(lane < LANES - shift, piece, more)
                    pair.append(piece)
                keep_ref[y, z, bucket] = jnp.where(core == 0, pair[0], pair[1]).astype(BF16)
                send_ref[y, z, bucket] = jnp.where(core == 0, pair[1], pair[0]).astype(BF16)


def grads(share, above, hidden):
    return pl.pallas_call(
        grad_kernel,
        out_shape=[shaped((YS, ZS, BUCKETS, RANK, LANES), BF16)] * 2,
        in_specs=[VMEM] * 9,
        out_specs=[VMEM] * 2,
        scratch_shapes=[pltpu.VMEM((RANK, BUCKET_ROWS), F32)],
        compiler_params=params(14),
        name="grads",
    )(*share, above, *hidden)


def core_sum_kernel(keep_ref, got_ref, own_ref, *outs):
    here = y_pos()
    own_ref[...] = keep_ref[here].astype(F32) + got_ref[here].astype(F32)
    for k, out in enumerate(outs):
        there = lax.rem(here + k + 1, YS)
        out[...] = (keep_ref[there].astype(F32) + got_ref[there].astype(F32)).astype(BF16)


def core_sum(keep, got):
    block = (ZS, BUCKETS, RANK, LANES)
    return pl.pallas_call(
        core_sum_kernel,
        out_shape=[shaped(block, F32)] + [shaped(block, BF16)] * 3,
        in_specs=[VMEM] * 2,
        out_specs=[VMEM] * 4,
        compiler_params=params(),
        name="core_sum",
    )(keep, got)


def y_sum_kernel(own_ref, g1, g2, g3, out_own, *outs):
    here = z_pos()
    for k, out in enumerate((out_own, *outs)):
        for far in range(2):
            z = here ^ (k + 4 * far)
            total = own_ref[z] + g1[z].astype(F32) + g2[z].astype(F32) + g3[z].astype(F32)
            out[far] = total.astype(out.dtype)


def y_sum(own, got):
    block = (2, BUCKETS, RANK, LANES)
    return pl.pallas_call(
        y_sum_kernel,
        out_shape=[shaped(block, F32)] + [shaped(block, BF16)] * 3,
        in_specs=[VMEM] * 4,
        out_specs=[VMEM] * 4,
        compiler_params=params(8),
        name="y_sum",
    )(own, *got)


def z_sum_kernel(own_ref, g1, g2, g3, out_own, out_far):
    total = [
        own_ref[far] + g1[far].astype(F32) + g2[far].astype(F32) + g3[far].astype(F32)
        for far in range(2)
    ]
    out_own[...] = total[0]
    out_far[...] = total[1].astype(BF16)


def z_sum(own, got):
    block = (BUCKETS, RANK, LANES)
    return pl.pallas_call(
        z_sum_kernel,
        out_shape=[shaped(block, F32), shaped(block, BF16)],
        in_specs=[VMEM] * 4,
        out_specs=[VMEM] * 2,
        compiler_params=params(4),
        name="z_sum",
    )(own, *got)


def adamw_kernel(own_ref, got_ref, master, moment, second, *outs):
    weight_out, master_out, moment_out, second_out = outs
    gradient = (own_ref[...] + got_ref[...].astype(F32))[:, :, 0:OWNED]
    weights = master[...]
    first_new = BETA_ONE * moment[...] + (1.0 - BETA_ONE) * gradient
    second_new = BETA_TWO * second[...] + (1.0 - BETA_TWO) * gradient * gradient
    first_hat = first_new / (1.0 - BETA_ONE**STEP)
    second_hat = second_new / (1.0 - BETA_TWO**STEP)
    weights_new = weights - LEARN_RATE * (
        first_hat / (jnp.sqrt(second_hat) + EPSILON) + DECAY_RATE * weights
    )
    weight_out[...] = jnp.zeros_like(weight_out)
    weight_out[:, :, 0:OWNED] = weights_new.astype(BF16)
    master_out[...] = weights_new
    moment_out[...] = first_new
    second_out[...] = second_new


def adamw(own, got, master, moment, second):
    state = shaped((BUCKETS, RANK, OWNED), F32)
    return pl.pallas_call(
        adamw_kernel,
        out_shape=[shaped((BUCKETS, RANK, LANES), BF16)] + [state] * 3,
        in_specs=[VMEM] * 5,
        out_specs=[VMEM] * 4,
        compiler_params=params(4),
        name="adamw",
    )(own, got, master, moment, second)


def assemble_kernel(*refs):
    arrays, (out_ref, blocks, sems) = refs[:8], refs[8:]
    core, y_here, z_here = core_pos(), y_pos(), z_pos()
    copies = []
    for side in range(2):
        for k in range(YS):
            copies.append(
                pltpu.make_async_copy(
                    arrays[side * YS + k],
                    blocks.at[lax.rem(core + side, 2), lax.rem(y_here + YS - k, YS)],
                    sems.at[side * YS + k],
                )
            )
            copies[-1].start()
    for copy in copies:
        copy.wait()
    lane = lax.broadcasted_iota(jnp.int32, (RANK, LANES), 1)
    places = [2 * ((z_here ^ z) & 3) + ((z_here ^ z) >> 2) for z in range(ZS)]
    for tile in range(FF // LANES):
        value = None
        first = tile * LANES // OWNED
        last = (tile * LANES + LANES - 1) // OWNED
        for piece in range(first, last + 1):
            bucket, owner = divmod(piece, 64)
            z, y, c = owner // 8, owner // 2 % YS, owner % 2
            block = blocks[c, y, places[z], bucket].astype(F32)
            start = piece * OWNED - tile * LANES
            if start % LANES:
                block = pltpu.roll(block, start % LANES, 1)
            value = block if value is None else jnp.where(lane < start, value, block)
        out_ref[:, tile * LANES : (tile + 1) * LANES] = value.astype(BF16)


def assemble(arrays):
    return pl.pallas_call(
        assemble_kernel,
        out_shape=shaped((RANK, FF), BF16),
        in_specs=[ANY] * 8,
        out_specs=VMEM,
        scratch_shapes=[
            pltpu.VMEM((2, YS, ZS, BUCKETS, RANK, LANES), BF16),
            pltpu.SemaphoreType.DMA((8,)),
        ],
        compiler_params=params(),
        name="assemble",
    )(*arrays)


def per_device(out_grad, pre_act, down_a, down_b, up_a, up_b, master, moment, second):
    da, ub = down_a[0].T, up_b[0].T
    mine = slices(down_b[0], up_a[0].T)
    ws = [mine[0]] + [over_section(mine[k], k) for k in (1, 2, 3)]
    slope = activation(pre_act[0])
    ws, slope = lax.optimization_barrier((ws, slope))
    share = shares(out_grad, ws)
    share = [share[0]] + [over_section(share[k], -k) for k in (1, 2, 3)]
    above, hidden, pre = None, [], pre_act[0]
    for i in range(3):
        sent = relay(share, above, slope, da, ub)
        above = lax.ppermute(sent, "section", [(1, 0), (2, 1), (3, 2)])
        if i < 2:
            pre, _ = lax.optimization_barrier((pre, sent))
            hidden += [activation(pre, 2 * i + b) for b in range(2)]
            above, *hidden = lax.optimization_barrier((above, *hidden))
    keep, send = grads(share, above, hidden)
    own, *sends = core_sum(keep, over_dp(send, dc=1))
    own, *sends = y_sum(own, [over_dp(sends[k - 1], dy=k) for k in (1, 2, 3)])
    own, send = z_sum(own, [over_dp(sends[k - 1], zx=k) for k in (1, 2, 3)])
    state = [a[0].transpose(0, 2, 1) for a in (master, moment, second)]
    weight, *state = adamw(own, over_dp(send, zx=4), *state)
    pair = jnp.stack([weight, over_dp(weight, zx=4)])
    column = jnp.concatenate([pair] + [over_dp(pair, zx=k) for k in (1, 2, 3)])
    plane = [column] + [over_dp(column, dy=k) for k in (1, 2, 3)]
    rows = assemble(plane + [over_dp(a, dc=1) for a in plane])
    return (rows.T[None], *[a.transpose(0, 2, 1)[None] for a in state])


def solution(mesh):
    return jax.shard_map(
        per_device,
        mesh=mesh,
        in_specs=(
            P("dp", "section"),
            P("section", "dp", None),
            P("section", None, None),
            P("section", None, None),
            P("section", None, None),
            P("section", None, None),
            P("section", None, "dp", None),
            P("section", None, "dp", None),
            P("section", None, "dp", None),
        ),
        out_specs=(
            P("section", None, None),
            P("section", None, "dp", None),
            P("section", None, "dp", None),
            P("section", None, "dp", None),
        ),
        check_vma=False,
    )
```

```python
import functools

import jax
import jax.numpy as jnp
from jax import lax
from jax.experimental import pallas as pl
from jax.experimental.pallas import tpu as pltpu
from jax.sharding import PartitionSpec as P

BUCKETS = 4
STEP = 20
BETA_ONE = 0.8
BETA_TWO = 0.95
LEARN_RATE = 0.02
DECAY_RATE = 0.1
EPSILON = 1e-08

TOKENS = 128
FF = 27648
RANK = 32
MODEL = 5120
WIDTH = MODEL // 4
BUCKET_ROWS = FF // BUCKETS
OWNED = 108
LANES = 128
ZS, YS = 8, 4
Y_ORDER = (0, 2, 3, 1)
BF16, F32 = jnp.bfloat16, jnp.float32
VMEM = pl.BlockSpec(memory_space=pltpu.VMEM)
ANY = pl.BlockSpec(memory_space=pl.ANY)
HBM = pl.BlockSpec(memory_space=pltpu.HBM)
CONTRACT_LAST = (((1,), (1,)), ((), ()))


def params(mib=16):
    return pltpu.CompilerParams(vmem_limit_bytes=mib * 1024 * 1024)


def in_hbm(array):
    return pltpu.with_memory_space_constraint(array, pltpu.HBM)


def shaped(shape, dtype):
    return jax.ShapeDtypeStruct(shape, dtype)


def z_pos():
    return lax.axis_index("dp") // 8


def y_pos():
    return (lax.axis_index("dp") // 2) % YS


def core_pos():
    return lax.axis_index("dp") % 2


def over_dp(value, zx=0, dy=0, dc=0):
    pairs = []
    for z in range(ZS):
        for y in range(YS):
            for c in range(2):
                target = (z ^ zx) * 8 + ((y + dy) % YS) * 2 + (c + dc) % 2
                pairs.append((z * 8 + y * 2 + c, target))
    return lax.ppermute(value, "dp", pairs)


def over_section(value, steps):
    return lax.ppermute(value, "section", [(i, (i + steps) % 4) for i in range(4)])


def slice_kernel(db_ref, ua_ref, *refs):
    outs, sems = refs[:4], refs[4]
    here = lax.axis_index("section")
    copies = []
    for k, out in enumerate(outs):
        columns = pl.ds(pl.multiple_of(lax.rem(here + k, 4) * WIDTH, LANES), WIDTH)
        for i, ref in enumerate((db_ref, ua_ref)):
            copies.append(
                pltpu.make_async_copy(
                    ref.at[:, columns], out.at[pl.ds(i * RANK, RANK), :], sems.at[2 * k + i]
                )
            )
            copies[-1].start()
    for copy in copies:
        copy.wait()


def slices(db, ua):
    return pl.pallas_call(
        slice_kernel,
        out_shape=[shaped((2 * RANK, WIDTH), BF16)] * 4,
        in_specs=[HBM] * 2,
        out_specs=[VMEM] * 4,
        scratch_shapes=[pltpu.SemaphoreType.DMA((8,))],
        compiler_params=params(4),
        name="slices",
    )(in_hbm(db), in_hbm(ua))


def activation_kernel(slope, first, parts, pre_ref, out_ref, held, sems):
    size = held.shape[1] // parts
    copies = []
    for i in range(parts):
        copies.append(
            pltpu.make_async_copy(
                pre_ref.at[:, pl.ds(first + i * size, size)],
                held.at[:, pl.ds(i * size, size)],
                sems.at[i],
            )
        )
        copies[-1].start()

    def chunk(i, _):
        columns = pl.ds(pl.multiple_of(i * 256, 256), 256)
        for row in range(0, TOKENS, 32):
            rows = slice(row, row + 32)
            half = 0.5 * held[rows, columns].astype(F32)
            t = jnp.tanh(half)
            h = half + half * t
            if slope:
                h = 0.5 * ((1.0 + t) + h * (1.0 - t))
            out_ref[rows, columns] = h.astype(BF16)
        return 0

    for i, copy in enumerate(copies):
        copy.wait()
        lax.fori_loop(i * size // 256, (i + 1) * size // 256, chunk, 0)


def activation(pre, slope, bucket, count=1):
    width, parts = BUCKET_ROWS * count, 3 * count
    return pl.pallas_call(
        functools.partial(activation_kernel, slope, bucket * BUCKET_ROWS, parts),
        out_shape=shaped((TOKENS, width), BF16),
        in_specs=[HBM],
        out_specs=VMEM,
        scratch_shapes=[
            pltpu.VMEM((TOKENS, width), BF16),
            pltpu.SemaphoreType.DMA((parts,)),
        ],
        compiler_params=params(4 * count + 2),
        cost_estimate=pl.CostEstimate(
            flops=10 * TOKENS * width,
            bytes_accessed=4 * TOKENS * width,
            transcendentals=TOKENS * width,
        ),
        name="slope" if slope else "hidden",
    )(in_hbm(pre))


def share_kernel(g_ref, w0, w1, w2, w3, *outs):
    ws = (w0, w1, w2, w3)
    for k, out in enumerate(outs):
        db = ws[k][0:RANK, :]
        out[:, 0:LANES] = lax.dot_general(
            db, g_ref[...], CONTRACT_LAST, preferred_element_type=F32
        )
        rows = jnp.concatenate([ws[(k - m) % 4][RANK:, :] for m in (1, 2, 3, 0)], axis=0)
        out[:, LANES:] = lax.dot_general(db, rows, CONTRACT_LAST, preferred_element_type=F32)


def shares(g, ws):
    return pl.pallas_call(
        share_kernel,
        out_shape=[shaped((RANK, 2 * LANES), F32)] * 4,
        in_specs=[VMEM] * 5,
        out_specs=[VMEM] * 4,
        compiler_params=params(),
        name="shares",
    )(g, *ws)


def low_of(share_refs, above_ref):
    total = share_refs[0][...] + share_refs[1][...] + share_refs[2][...] + share_refs[3][...]
    low = total[:, 0:LANES]
    if above_ref is not None:
        low = low + jnp.dot(
            total[:, LANES : LANES + 3 * RANK],
            above_ref[...].astype(F32),
            preferred_element_type=F32,
            precision=lax.Precision.HIGHEST,
        )
    return low


def relay_kernel(top, *refs):
    share_refs, refs = refs[:4], refs[4:]
    above_ref = None
    if not top:
        above_ref, refs = refs[0], refs[1:]
    slope_refs, (da_ref, ub_ref, out_ref) = refs[:2], refs[2:]
    low = low_of(share_refs, above_ref).T.astype(BF16)
    total = jnp.zeros((RANK, TOKENS), F32)

    start = 0
    for slope_ref in slope_refs:
        for first in range(0, slope_ref.shape[1], 768):
            columns = slice(start, start + 768)
            upstream = jnp.dot(low, da_ref[:, columns], preferred_element_type=F32)
            slope = slope_ref[:, first : first + 768].astype(F32)
            delta = (upstream * slope).astype(BF16)
            total = total + lax.dot_general(
                ub_ref[:, columns], delta, CONTRACT_LAST, preferred_element_type=F32
            )
            start += 768
    out_ref[0:RANK, :] = total.astype(BF16)
    if top:
        out_ref[RANK:, :] = jnp.zeros((2 * RANK, LANES), BF16)
    else:
        out_ref[RANK:, :] = above_ref[0 : 2 * RANK, :]


def relay(share, above, slope, da, ub):
    first = above is None
    return pl.pallas_call(
        functools.partial(relay_kernel, first),
        out_shape=shaped((3 * RANK, LANES), BF16),
        in_specs=[VMEM] * (8 if first else 9),
        out_specs=VMEM,
        compiler_params=params(14),
        name="relay_first" if first else "relay",
    )(*share, *([] if first else [above]), *slope, da, ub)


def grad_kernel(s0, s1, s2, s3, above_ref, h0, h1, h2, h3, keep_ref, send_ref, grad):
    low = low_of((s0, s1, s2, s3), above_ref).astype(BF16)
    core = core_pos()
    lane = lax.broadcasted_iota(jnp.int32, (RANK, LANES), 1)
    for bucket, hidden_ref in enumerate((h0, h1, h2, h3)):
        grad[...] = jnp.dot(low, hidden_ref[...], preferred_element_type=F32)
        for z in range(ZS):
            for y in range(YS):
                pair = []
                for c in range(2):
                    start = (z * 8 + y * 2 + c) * OWNED
                    base, shift = start // LANES * LANES, start % LANES
                    piece = grad[:, base : base + LANES]
                    if shift:
                        piece = pltpu.roll(piece, LANES - shift, 1)
                    if shift + OWNED > LANES:
                        more = pltpu.roll(
                            grad[:, base + LANES : base + 2 * LANES], LANES - shift, 1
                        )
                        piece = jnp.where(lane < LANES - shift, piece, more)
                    pair.append(piece)
                keep_ref[y, z, bucket] = jnp.where(core == 0, pair[0], pair[1]).astype(BF16)
                send_ref[y, z, bucket] = jnp.where(core == 0, pair[1], pair[0]).astype(BF16)


def grads(share, above, hidden):
    return pl.pallas_call(
        grad_kernel,
        out_shape=[shaped((YS, ZS, BUCKETS, RANK, LANES), BF16)] * 2,
        in_specs=[VMEM] * 9,
        out_specs=[VMEM] * 2,
        scratch_shapes=[pltpu.VMEM((RANK, BUCKET_ROWS), F32)],
        compiler_params=params(14),
        name="grads",
    )(*share, above, *hidden)


def core_sum_kernel(keep_ref, got_ref, own_ref, *outs):
    here = y_pos()
    own_ref[...] = keep_ref[here].astype(F32) + got_ref[here].astype(F32)
    for k, out in enumerate(outs):
        there = lax.rem(here + k + 1, YS)
        out[...] = (keep_ref[there].astype(F32) + got_ref[there].astype(F32)).astype(BF16)


def core_sum(keep, got):
    block = (ZS, BUCKETS, RANK, LANES)
    return pl.pallas_call(
        core_sum_kernel,
        out_shape=[shaped(block, F32)] + [shaped(block, BF16)] * 3,
        in_specs=[VMEM] * 2,
        out_specs=[VMEM] * 4,
        compiler_params=params(),
        name="core_sum",
    )(keep, got)


def y_sum_kernel(own_ref, g1, g2, g3, out_own, *outs):
    here = z_pos()
    for k, out in enumerate((out_own, *outs)):
        for far in range(2):
            z = here ^ (k + 4 * far)
            total = own_ref[z] + g1[z].astype(F32) + g2[z].astype(F32) + g3[z].astype(F32)
            out[far] = total.astype(out.dtype)


def y_sum(own, got):
    block = (2, BUCKETS, RANK, LANES)
    return pl.pallas_call(
        y_sum_kernel,
        out_shape=[shaped(block, F32)] + [shaped(block, BF16)] * 3,
        in_specs=[VMEM] * 4,
        out_specs=[VMEM] * 4,
        compiler_params=params(8),
        name="y_sum",
    )(own, *got)


def z_sum_kernel(own_ref, g1, g2, g3, out_own, out_far):
    total = [
        own_ref[far] + g1[far].astype(F32) + g2[far].astype(F32) + g3[far].astype(F32)
        for far in range(2)
    ]
    out_own[...] = total[0]
    out_far[...] = total[1].astype(BF16)


def z_sum(own, got):
    block = (BUCKETS, RANK, LANES)
    return pl.pallas_call(
        z_sum_kernel,
        out_shape=[shaped(block, F32), shaped(block, BF16)],
        in_specs=[VMEM] * 4,
        out_specs=[VMEM] * 2,
        compiler_params=params(4),
        name="z_sum",
    )(own, *got)


def adamw_kernel(own_ref, got_ref, master, moment, second, *outs):
    weight_out, master_out, moment_out, second_out = outs
    gradient = (own_ref[...] + got_ref[...].astype(F32))[:, :, 0:OWNED]
    weights = master[...]
    first_new = BETA_ONE * moment[...] + (1.0 - BETA_ONE) * gradient
    second_new = BETA_TWO * second[...] + (1.0 - BETA_TWO) * gradient * gradient
    first_hat = first_new / (1.0 - BETA_ONE**STEP)
    second_hat = second_new / (1.0 - BETA_TWO**STEP)
    weights_new = weights - LEARN_RATE * (
        first_hat / (jnp.sqrt(second_hat) + EPSILON) + DECAY_RATE * weights
    )
    weight_out[...] = jnp.zeros_like(weight_out)
    weight_out[:, :, 0:OWNED] = weights_new.astype(BF16)
    master_out[...] = weights_new
    moment_out[...] = first_new
    second_out[...] = second_new


def adamw(own, got, master, moment, second):
    state = shaped((BUCKETS, RANK, OWNED), F32)
    return pl.pallas_call(
        adamw_kernel,
        out_shape=[shaped((BUCKETS, RANK, LANES), BF16)] + [state] * 3,
        in_specs=[VMEM] * 5,
        out_specs=[VMEM] * 4,
        compiler_params=params(4),
        name="adamw",
    )(own, got, master, moment, second)


def assemble_kernel(*refs):
    arrays, (out_ref, blocks, sems) = refs[:8], refs[8:]
    core, y_here, z_here = core_pos(), y_pos(), z_pos()
    copies = []
    for side in range(2):
        for i, k in enumerate(Y_ORDER):
            copies.append(
                pltpu.make_async_copy(
                    arrays[side * YS + i],
                    blocks.at[lax.rem(core + side, 2), lax.rem(y_here + YS - k, YS)],
                    sems.at[side * YS + i],
                )
            )
            copies[-1].start()
    for copy in copies:
        copy.wait()
    lane = lax.broadcasted_iota(jnp.int32, (RANK, LANES), 1)
    places = [2 * ((z_here ^ z) & 3) + ((z_here ^ z) >> 2) for z in range(ZS)]
    for tile in range(FF // LANES):
        value = None
        first = tile * LANES // OWNED
        last = (tile * LANES + LANES - 1) // OWNED
        for piece in range(first, last + 1):
            bucket, owner = divmod(piece, 64)
            z, y, c = owner // 8, owner // 2 % YS, owner % 2
            block = blocks[c, y, places[z], bucket].astype(F32)
            start = piece * OWNED - tile * LANES
            if start % LANES:
                block = pltpu.roll(block, start % LANES, 1)
            value = block if value is None else jnp.where(lane < start, value, block)
        out_ref[:, tile * LANES : (tile + 1) * LANES] = value.astype(BF16)


def assemble(arrays):
    return pl.pallas_call(
        assemble_kernel,
        out_shape=shaped((RANK, FF), BF16),
        in_specs=[ANY] * 8,
        out_specs=VMEM,
        scratch_shapes=[
            pltpu.VMEM((2, YS, ZS, BUCKETS, RANK, LANES), BF16),
            pltpu.SemaphoreType.DMA((8,)),
        ],
        compiler_params=params(),
        name="assemble",
    )(*arrays)


def per_device(out_grad, pre_act, down_a, down_b, up_a, up_b, master, moment, second):
    da, ub = down_a[0].T, up_b[0].T
    mine = slices(down_b[0], up_a[0].T)
    ws = [mine[0]] + [over_section(mine[k], k) for k in (1, 3, 2)]
    pre = pre_act[0]
    slope = activation(pre, True, 0, 3)
    ws, slope = lax.optimization_barrier((ws, slope))
    share = shares(out_grad, [ws[0], ws[1], ws[3], ws[2]])
    pre, _ = lax.optimization_barrier((pre, share[0]))
    slope = [slope, activation(pre, True, 3)]
    share = [share[0]] + [over_section(share[k], -k) for k in (1, 3, 2)]
    above, hidden = None, []
    for i in range(3):
        sent = relay(share, above, slope, da, ub)
        above = lax.ppermute(sent, "section", [(1, 0), (2, 1), (3, 2)])
        if i < 2:
            pre, _ = lax.optimization_barrier((pre, sent))
            hidden += [activation(pre, False, 2 * i + b) for b in range(2)]
            above, *hidden = lax.optimization_barrier((above, *hidden))
    keep, send = grads(share, above, hidden)
    own, *sends = core_sum(keep, over_dp(send, dc=1))
    own, *sends = y_sum(own, [over_dp(sends[k - 1], dy=k) for k in (1, 3, 2)])
    own, send = z_sum(own, [over_dp(sends[k - 1], zx=k) for k in (3, 2, 1)])
    state = [a[0].transpose(0, 2, 1) for a in (master, moment, second)]
    weight, *state = adamw(own, over_dp(send, zx=4), *state)
    pair = jnp.stack([weight, over_dp(weight, zx=4)])
    column = jnp.concatenate([pair] + [over_dp(pair, zx=k) for k in (1, 2, 3)])
    plane = [column] + [over_dp(column, dy=k) for k in Y_ORDER[1:]]
    rows = assemble(plane + [over_dp(a, dc=1) for a in plane])
    return (rows.T[None], *[a.transpose(0, 2, 1)[None] for a in state])


def solution(mesh):
    return jax.shard_map(
        per_device,
        mesh=mesh,
        in_specs=(
            P("dp", "section"),
            P("section", "dp", None),
            P("section", None, None),
            P("section", None, None),
            P("section", None, None),
            P("section", None, None),
            P("section", None, "dp", None),
            P("section", None, "dp", None),
            P("section", None, "dp", None),
        ),
        out_specs=(
            P("section", None, None),
            P("section", None, "dp", None),
            P("section", None, "dp", None),
            P("section", None, "dp", None),
        ),
        check_vma=False,
    )
```

```python
import functools

import jax
import jax.numpy as jnp
from jax import lax
from jax.experimental import pallas as pl
from jax.experimental.pallas import tpu as pltpu
from jax.sharding import PartitionSpec as P

BUCKETS = 4
STEP = 20
BETA_ONE = 0.8
BETA_TWO = 0.95
LEARN_RATE = 0.02
DECAY_RATE = 0.1
EPSILON = 1e-08

TOKENS = 128
FF = 27648
RANK = 32
MODEL = 5120
WIDTH = MODEL // 4
BUCKET_ROWS = FF // BUCKETS
OWNED = 108
LANES = 128
ZS, YS = 8, 4
Z_STEPS = (5, 6, 2)
Y_ORDER = (0, 2, 3, 1)
BF16, F32 = jnp.bfloat16, jnp.float32
VMEM = pl.BlockSpec(memory_space=pltpu.VMEM)
ANY = pl.BlockSpec(memory_space=pl.ANY)
HBM = pl.BlockSpec(memory_space=pltpu.HBM)
CONTRACT_LAST = (((1,), (1,)), ((), ()))


def params(mib=16):
    return pltpu.CompilerParams(vmem_limit_bytes=mib * 1024 * 1024)


def in_hbm(array):
    return pltpu.with_memory_space_constraint(array, pltpu.HBM)


def shaped(shape, dtype):
    return jax.ShapeDtypeStruct(shape, dtype)


def z_pos():
    return lax.axis_index("dp") // 8


def y_pos():
    return (lax.axis_index("dp") // 2) % YS


def core_pos():
    return lax.axis_index("dp") % 2


def over_dp(value, zx=0, dy=0, dc=0):
    pairs = []
    for z in range(ZS):
        for y in range(YS):
            for c in range(2):
                target = (z ^ zx) * 8 + ((y + dy) % YS) * 2 + (c + dc) % 2
                pairs.append((z * 8 + y * 2 + c, target))
    return lax.ppermute(value, "dp", pairs)


def over_section(value, steps):
    return lax.ppermute(value, "section", [(i, (i + steps) % 4) for i in range(4)])


def slice_kernel(db_ref, ua_ref, *refs):
    outs, sems = refs[:4], refs[4]
    here = lax.axis_index("section")
    copies = []
    for k, out in enumerate(outs):
        columns = pl.ds(pl.multiple_of(lax.rem(here + k, 4) * WIDTH, LANES), WIDTH)
        for i, ref in enumerate((db_ref, ua_ref)):
            copies.append(
                pltpu.make_async_copy(
                    ref.at[:, columns], out.at[pl.ds(i * RANK, RANK), :], sems.at[2 * k + i]
                )
            )
            copies[-1].start()
    for copy in copies:
        copy.wait()


def slices(db, ua):
    return pl.pallas_call(
        slice_kernel,
        out_shape=[shaped((2 * RANK, WIDTH), BF16)] * 4,
        in_specs=[HBM] * 2,
        out_specs=[VMEM] * 4,
        scratch_shapes=[pltpu.SemaphoreType.DMA((8,))],
        compiler_params=params(4),
        name="slices",
    )(in_hbm(db), in_hbm(ua))


def activation_kernel(slope, first, parts, pre_ref, out_ref, held, sems):
    size = held.shape[1] // parts
    copies = []
    for i in range(parts):
        copies.append(
            pltpu.make_async_copy(
                pre_ref.at[:, pl.ds(first + i * size, size)],
                held.at[:, pl.ds(i * size, size)],
                sems.at[i],
            )
        )
        copies[-1].start()

    def chunk(i, _):
        columns = pl.ds(pl.multiple_of(i * 256, 256), 256)
        for row in range(0, TOKENS, 32):
            rows = slice(row, row + 32)
            half = 0.5 * held[rows, columns].astype(F32)
            t = jnp.tanh(half)
            h = half + half * t
            if slope:
                h = (1.0 + t) + h * (1.0 - t)
            out_ref[rows, columns] = h.astype(BF16)
        return 0

    for i, copy in enumerate(copies):
        copy.wait()
        lax.fori_loop(i * size // 256, (i + 1) * size // 256, chunk, 0)


def activation(pre, slope, bucket, count=1):
    width, parts = BUCKET_ROWS * count, 3 * count
    return pl.pallas_call(
        functools.partial(activation_kernel, slope, bucket * BUCKET_ROWS, parts),
        out_shape=shaped((TOKENS, width), BF16),
        in_specs=[HBM],
        out_specs=VMEM,
        scratch_shapes=[
            pltpu.VMEM((TOKENS, width), BF16),
            pltpu.SemaphoreType.DMA((parts,)),
        ],
        compiler_params=params(4 * count + 2),
        cost_estimate=pl.CostEstimate(
            flops=10 * TOKENS * width,
            bytes_accessed=4 * TOKENS * width,
            transcendentals=TOKENS * width,
        ),
        name="slope" if slope else "hidden",
    )(in_hbm(pre))


def share_kernel(g_ref, w0, w1, w2, w3, *outs):
    ws = (w0, w1, w2, w3)
    for k, out in enumerate(outs):
        db = ws[k][0:RANK, :]
        out[:, 0:LANES] = lax.dot_general(
            db, g_ref[...], CONTRACT_LAST, preferred_element_type=F32
        )
        rows = jnp.concatenate([ws[(k - m) % 4][RANK:, :] for m in (1, 2, 3, 0)], axis=0)
        out[:, LANES:] = lax.dot_general(db, rows, CONTRACT_LAST, preferred_element_type=F32)


def shares(g, ws):
    return pl.pallas_call(
        share_kernel,
        out_shape=[shaped((RANK, 2 * LANES), F32)] * 4,
        in_specs=[VMEM] * 5,
        out_specs=[VMEM] * 4,
        compiler_params=params(),
        name="shares",
    )(g, *ws)


def low_of(share_refs, above_ref):
    total = share_refs[0][...] + share_refs[1][...] + share_refs[2][...] + share_refs[3][...]
    low = total[:, 0:LANES]
    if above_ref is not None:
        low = low + jnp.dot(
            total[:, LANES : LANES + 3 * RANK],
            above_ref[...].astype(F32),
            preferred_element_type=F32,
            precision=lax.Precision.HIGHEST,
        )
    return low


def relay_kernel(top, *refs):
    share_refs, refs = refs[:4], refs[4:]
    above_ref = None
    if not top:
        above_ref, refs = refs[0], refs[1:]
    slope_refs, (da_ref, ub_ref, out_ref) = refs[:2], refs[2:]
    low = low_of(share_refs, above_ref).T.astype(BF16)
    total = jnp.zeros((RANK, TOKENS), F32)

    start = 0
    for slope_ref in slope_refs:
        for first in range(0, slope_ref.shape[1], 768):
            columns = slice(start, start + 768)
            upstream = jnp.dot(low, da_ref[:, columns], preferred_element_type=F32)
            slope = slope_ref[:, first : first + 768].astype(F32)
            delta = (upstream * slope).astype(BF16)
            total = total + lax.dot_general(
                ub_ref[:, columns], delta, CONTRACT_LAST, preferred_element_type=F32
            )
            start += 768
    out_ref[0:RANK, :] = (0.5 * total).astype(BF16)
    if top:
        out_ref[RANK:, :] = jnp.zeros((2 * RANK, LANES), BF16)
    else:
        out_ref[RANK:, :] = above_ref[0 : 2 * RANK, :]


def relay(share, above, slope, da, ub):
    first = above is None
    return pl.pallas_call(
        functools.partial(relay_kernel, first),
        out_shape=shaped((3 * RANK, LANES), BF16),
        in_specs=[VMEM] * (8 if first else 9),
        out_specs=VMEM,
        compiler_params=params(14),
        name="relay_first" if first else "relay",
    )(*share, *([] if first else [above]), *slope, da, ub)


def grad_kernel(s0, s1, s2, s3, above_ref, h0, h1, h2, h3, keep_ref, send_ref, grad):
    low = low_of((s0, s1, s2, s3), above_ref).astype(BF16)
    core = core_pos()
    lane = lax.broadcasted_iota(jnp.int32, (RANK, LANES), 1)
    for bucket, hidden_ref in enumerate((h0, h1, h2, h3)):
        grad[...] = jnp.dot(low, hidden_ref[...], preferred_element_type=F32)
        for z in range(ZS):
            for y in range(YS):
                pair = []
                for c in range(2):
                    start = (z * 8 + y * 2 + c) * OWNED
                    base, shift = start // LANES * LANES, start % LANES
                    piece = grad[:, base : base + LANES]
                    if shift:
                        piece = pltpu.roll(piece, LANES - shift, 1)
                    if shift + OWNED > LANES:
                        more = pltpu.roll(
                            grad[:, base + LANES : base + 2 * LANES], LANES - shift, 1
                        )
                        piece = jnp.where(lane < LANES - shift, piece, more)
                    pair.append(piece)
                keep_ref[y, z, bucket] = jnp.where(core == 0, pair[0], pair[1]).astype(BF16)
                send_ref[y, z, bucket] = jnp.where(core == 0, pair[1], pair[0]).astype(BF16)


def grads(share, above, hidden):
    return pl.pallas_call(
        grad_kernel,
        out_shape=[shaped((YS, ZS, BUCKETS, RANK, LANES), BF16)] * 2,
        in_specs=[VMEM] * 9,
        out_specs=[VMEM] * 2,
        scratch_shapes=[pltpu.VMEM((RANK, BUCKET_ROWS), F32)],
        compiler_params=params(14),
        name="grads",
    )(*share, above, *hidden)


def core_sum_kernel(keep_ref, got_ref, own_ref, *outs):
    here = y_pos()
    own_ref[...] = keep_ref[here].astype(F32) + got_ref[here].astype(F32)
    for k, out in enumerate(outs):
        there = lax.rem(here + k + 1, YS)
        out[...] = (keep_ref[there].astype(F32) + got_ref[there].astype(F32)).astype(BF16)


def core_sum(keep, got):
    block = (ZS, BUCKETS, RANK, LANES)
    return pl.pallas_call(
        core_sum_kernel,
        out_shape=[shaped(block, F32)] + [shaped(block, BF16)] * 3,
        in_specs=[VMEM] * 2,
        out_specs=[VMEM] * 4,
        compiler_params=params(),
        name="core_sum",
    )(keep, got)


def y_sum_kernel(own_ref, g1, g2, g3, out_own, *outs):
    here = z_pos()
    for step, out in zip((0, *Z_STEPS), (out_own, *outs)):
        for far in range(2):
            z = here ^ (step ^ far)
            total = own_ref[z] + g1[z].astype(F32) + g2[z].astype(F32) + g3[z].astype(F32)
            out[far] = total.astype(out.dtype)


def y_sum(own, got):
    block = (2, BUCKETS, RANK, LANES)
    return pl.pallas_call(
        y_sum_kernel,
        out_shape=[shaped(block, F32)] + [shaped(block, BF16)] * 3,
        in_specs=[VMEM] * 4,
        out_specs=[VMEM] * 4,
        compiler_params=params(8),
        name="y_sum",
    )(own, *got)


def z_sum_kernel(own_ref, g1, g2, g3, out_own, out_far):
    total = [
        own_ref[far] + g1[far].astype(F32) + g2[far].astype(F32) + g3[far].astype(F32)
        for far in range(2)
    ]
    out_own[...] = total[0]
    out_far[...] = total[1].astype(BF16)


def z_sum(own, got):
    block = (BUCKETS, RANK, LANES)
    return pl.pallas_call(
        z_sum_kernel,
        out_shape=[shaped(block, F32), shaped(block, BF16)],
        in_specs=[VMEM] * 4,
        out_specs=[VMEM] * 2,
        compiler_params=params(4),
        name="z_sum",
    )(own, *got)


def adamw_kernel(own_ref, got_ref, master, moment, second, *outs):
    weight_out, master_out, moment_out, second_out = outs
    gradient = (own_ref[...] + got_ref[...].astype(F32))[:, :, 0:OWNED]
    weights = master[...]
    first_new = BETA_ONE * moment[...] + (1.0 - BETA_ONE) * gradient
    second_new = BETA_TWO * second[...] + (1.0 - BETA_TWO) * gradient * gradient
    first_hat = first_new / (1.0 - BETA_ONE**STEP)
    second_hat = second_new / (1.0 - BETA_TWO**STEP)
    weights_new = weights - LEARN_RATE * (
        first_hat / (jnp.sqrt(second_hat) + EPSILON) + DECAY_RATE * weights
    )
    weight_out[...] = jnp.zeros_like(weight_out)
    weight_out[:, :, 0:OWNED] = weights_new.astype(BF16)
    master_out[...] = weights_new
    moment_out[...] = first_new
    second_out[...] = second_new


def adamw(own, got, master, moment, second):
    state = shaped((BUCKETS, RANK, OWNED), F32)
    return pl.pallas_call(
        adamw_kernel,
        out_shape=[shaped((BUCKETS, RANK, LANES), BF16)] + [state] * 3,
        in_specs=[VMEM] * 5,
        out_specs=[VMEM] * 4,
        compiler_params=params(4),
        name="adamw",
    )(own, got, master, moment, second)


def assemble_kernel(*refs):
    arrays, (out_ref, blocks, sems) = refs[:8], refs[8:]
    core, y_here, z_here = core_pos(), y_pos(), z_pos()
    copies = []
    for side in range(2):
        for i, k in enumerate(Y_ORDER):
            copies.append(
                pltpu.make_async_copy(
                    arrays[side * YS + i],
                    blocks.at[lax.rem(core + side, 2), lax.rem(y_here + YS - k, YS)],
                    sems.at[side * YS + i],
                )
            )
            copies[-1].start()
    for copy in copies:
        copy.wait()
    lane = lax.broadcasted_iota(jnp.int32, (RANK, LANES), 1)
    apart = [z_here ^ z for z in range(ZS)]
    places = [
        jnp.where(a < 4, a, jnp.where(a < 6, 11 - a, a - 2)) for a in apart
    ]
    for tile in range(FF // LANES):
        value = None
        first = tile * LANES // OWNED
        last = (tile * LANES + LANES - 1) // OWNED
        for piece in range(first, last + 1):
            bucket, owner = divmod(piece, 64)
            z, y, c = owner // 8, owner // 2 % YS, owner % 2
            block = blocks[c, y, places[z], bucket].astype(F32)
            start = piece * OWNED - tile * LANES
            if start % LANES:
                block = pltpu.roll(block, start % LANES, 1)
            value = block if value is None else jnp.where(lane < start, value, block)
        out_ref[:, tile * LANES : (tile + 1) * LANES] = value.astype(BF16)


def assemble(arrays):
    return pl.pallas_call(
        assemble_kernel,
        out_shape=shaped((RANK, FF), BF16),
        in_specs=[ANY] * 8,
        out_specs=VMEM,
        scratch_shapes=[
            pltpu.VMEM((2, YS, ZS, BUCKETS, RANK, LANES), BF16),
            pltpu.SemaphoreType.DMA((8,)),
        ],
        compiler_params=params(),
        name="assemble",
    )(*arrays)


def per_device(out_grad, pre_act, down_a, down_b, up_a, up_b, master, moment, second):
    da, ub = down_a[0].T, up_b[0].T
    mine = slices(down_b[0], up_a[0].T)
    ws = [mine[0]] + [over_section(mine[k], k) for k in (1, 3, 2)]
    pre = pre_act[0]
    slope = activation(pre, True, 0, 3)
    ws, slope = lax.optimization_barrier((ws, slope))
    share = shares(out_grad, [ws[0], ws[1], ws[3], ws[2]])
    pre, _ = lax.optimization_barrier((pre, share[0]))
    slope = [slope, activation(pre, True, 3)]
    share = [share[0]] + [over_section(share[k], -k) for k in (1, 3, 2)]
    above, hidden = None, []
    for i in range(3):
        sent = relay(share, above, slope, da, ub)
        above = lax.ppermute(sent, "section", [(1, 0), (2, 1), (3, 2)])
        if i < 2:
            pre, _ = lax.optimization_barrier((pre, sent))
            hidden += [activation(pre, False, 2 * i + b) for b in range(2)]
            above, *hidden = lax.optimization_barrier((above, *hidden))
    keep, send = grads(share, above, hidden)
    own, *sends = core_sum(keep, over_dp(send, dc=1))
    own, *sends = y_sum(own, [over_dp(sends[k - 1], dy=k) for k in (1, 3, 2)])
    own, send = z_sum(own, [over_dp(a, zx=k) for a, k in zip(sends, Z_STEPS)])
    state = [a[0].transpose(0, 2, 1) for a in (master, moment, second)]
    weight, *state = adamw(own, over_dp(send, zx=1), *state)
    pair = jnp.stack([weight, over_dp(weight, zx=1)])
    column = jnp.concatenate([pair] + [over_dp(pair, zx=k) for k in Z_STEPS[::-1]])
    plane = [column] + [over_dp(column, dy=k) for k in Y_ORDER[1:]]
    rows = assemble(plane + [over_dp(a, dc=1) for a in plane])
    return (rows.T[None], *[a.transpose(0, 2, 1)[None] for a in state])


def solution(mesh):
    return jax.shard_map(
        per_device,
        mesh=mesh,
        in_specs=(
            P("dp", "section"),
            P("section", "dp", None),
            P("section", None, None),
            P("section", None, None),
            P("section", None, None),
            P("section", None, None),
            P("section", None, "dp", None),
            P("section", None, "dp", None),
            P("section", None, "dp", None),
        ),
        out_specs=(
            P("section", None, None),
            P("section", None, "dp", None),
            P("section", None, "dp", None),
            P("section", None, "dp", None),
        ),
        check_vma=False,
    )
```

```python
import functools

import jax
import jax.numpy as jnp
from jax import lax
from jax.experimental import pallas as pl
from jax.experimental.pallas import tpu as pltpu
from jax.sharding import PartitionSpec as P

BUCKETS = 4
STEP = 20
BETA_ONE = 0.8
BETA_TWO = 0.95
LEARN_RATE = 0.02
DECAY_RATE = 0.1
EPSILON = 1e-08

TOKENS = 128
FF = 27648
RANK = 32
MODEL = 5120
WIDTH = MODEL // 4
BUCKET_ROWS = FF // BUCKETS
OWNED = 108
LANES = 128
ZS, YS = 8, 4
Z_STEPS = (3, 2, 1)
Z_PARTNER = 7
Y_ORDER = (0, 2, 3, 1)
BF16, F32 = jnp.bfloat16, jnp.float32
VMEM = pl.BlockSpec(memory_space=pltpu.VMEM)
ANY = pl.BlockSpec(memory_space=pl.ANY)
HBM = pl.BlockSpec(memory_space=pltpu.HBM)
CONTRACT_LAST = (((1,), (1,)), ((), ()))


def params(mib=16):
    return pltpu.CompilerParams(vmem_limit_bytes=mib * 1024 * 1024)


def in_hbm(array):
    return pltpu.with_memory_space_constraint(array, pltpu.HBM)


def shaped(shape, dtype):
    return jax.ShapeDtypeStruct(shape, dtype)


def z_pos():
    return lax.axis_index("dp") // 8


def y_pos():
    return (lax.axis_index("dp") // 2) % YS


def core_pos():
    return lax.axis_index("dp") % 2


def over_dp(value, zx=0, dy=0, dc=0):
    pairs = []
    for z in range(ZS):
        for y in range(YS):
            for c in range(2):
                target = (z ^ zx) * 8 + ((y + dy) % YS) * 2 + (c + dc) % 2
                pairs.append((z * 8 + y * 2 + c, target))
    return lax.ppermute(value, "dp", pairs)


def over_section(value, steps):
    return lax.ppermute(value, "section", [(i, (i + steps) % 4) for i in range(4)])


def slice_kernel(db_ref, ua_ref, *refs):
    outs, sems = refs[:4], refs[4]
    here = lax.axis_index("section")
    copies = []
    for k, out in enumerate(outs):
        columns = pl.ds(pl.multiple_of(lax.rem(here + k, 4) * WIDTH, LANES), WIDTH)
        for i, ref in enumerate((db_ref, ua_ref)):
            copies.append(
                pltpu.make_async_copy(
                    ref.at[:, columns], out.at[pl.ds(i * RANK, RANK), :], sems.at[2 * k + i]
                )
            )
            copies[-1].start()
    for copy in copies:
        copy.wait()


def slices(db, ua):
    return pl.pallas_call(
        slice_kernel,
        out_shape=[shaped((2 * RANK, WIDTH), BF16)] * 4,
        in_specs=[HBM] * 2,
        out_specs=[VMEM] * 4,
        scratch_shapes=[pltpu.SemaphoreType.DMA((8,))],
        compiler_params=params(4),
        name="slices",
    )(in_hbm(db), in_hbm(ua))


def activation_kernel(slope, first, parts, pre_ref, out_ref, held, sems):
    size = held.shape[1] // parts
    copies = []
    for i in range(parts):
        copies.append(
            pltpu.make_async_copy(
                pre_ref.at[:, pl.ds(first + i * size, size)],
                held.at[:, pl.ds(i * size, size)],
                sems.at[i],
            )
        )
        copies[-1].start()

    def chunk(i, _):
        columns = pl.ds(pl.multiple_of(i * 256, 256), 256)
        for row in range(0, TOKENS, 32):
            rows = slice(row, row + 32)
            half = 0.5 * held[rows, columns].astype(F32)
            t = jnp.tanh(half)
            h = half + half * t
            if slope:
                h = (1.0 + t) + h * (1.0 - t)
            out_ref[rows, columns] = h.astype(BF16)
        return 0

    for i, copy in enumerate(copies):
        copy.wait()
        lax.fori_loop(i * size // 256, (i + 1) * size // 256, chunk, 0)


def activation(pre, slope, bucket, count=1):
    width, parts = BUCKET_ROWS * count, 3 * count
    return pl.pallas_call(
        functools.partial(activation_kernel, slope, bucket * BUCKET_ROWS, parts),
        out_shape=shaped((TOKENS, width), BF16),
        in_specs=[HBM],
        out_specs=VMEM,
        scratch_shapes=[
            pltpu.VMEM((TOKENS, width), BF16),
            pltpu.SemaphoreType.DMA((parts,)),
        ],
        compiler_params=params(4 * count + 2),
        cost_estimate=pl.CostEstimate(
            flops=10 * TOKENS * width,
            bytes_accessed=4 * TOKENS * width,
            transcendentals=TOKENS * width,
        ),
        name="slope" if slope else "hidden",
    )(in_hbm(pre))


def share_kernel(g_ref, w0, w1, w2, w3, *outs):
    ws = (w0, w1, w2, w3)
    for k, out in enumerate(outs):
        db = ws[k][0:RANK, :]
        out[:, 0:LANES] = lax.dot_general(
            db, g_ref[...], CONTRACT_LAST, preferred_element_type=F32
        )
        rows = jnp.concatenate([ws[(k - m) % 4][RANK:, :] for m in (1, 2, 3, 0)], axis=0)
        out[:, LANES:] = lax.dot_general(db, rows, CONTRACT_LAST, preferred_element_type=F32)


def shares(g, ws):
    return pl.pallas_call(
        share_kernel,
        out_shape=[shaped((RANK, 2 * LANES), F32)] * 4,
        in_specs=[VMEM] * 5,
        out_specs=[VMEM] * 4,
        compiler_params=params(),
        name="shares",
    )(g, *ws)


def low_of(share_refs, above_ref):
    total = share_refs[0][...] + share_refs[1][...] + share_refs[2][...] + share_refs[3][...]
    low = total[:, 0:LANES]
    if above_ref is not None:
        low = low + jnp.dot(
            total[:, LANES : LANES + 3 * RANK],
            above_ref[...].astype(F32),
            preferred_element_type=F32,
            precision=lax.Precision.HIGHEST,
        )
    return low


def relay_kernel(top, *refs):
    share_refs, refs = refs[:4], refs[4:]
    above_ref = None
    if not top:
        above_ref, refs = refs[0], refs[1:]
    slope_refs, (da_ref, ub_ref, out_ref) = refs[:2], refs[2:]
    low = low_of(share_refs, above_ref).T.astype(BF16)
    total = jnp.zeros((RANK, TOKENS), F32)

    start = 0
    for slope_ref in slope_refs:
        for first in range(0, slope_ref.shape[1], 768):
            columns = slice(start, start + 768)
            upstream = jnp.dot(low, da_ref[:, columns], preferred_element_type=F32)
            slope = slope_ref[:, first : first + 768].astype(F32)
            delta = (upstream * slope).astype(BF16)
            total = total + lax.dot_general(
                ub_ref[:, columns], delta, CONTRACT_LAST, preferred_element_type=F32
            )
            start += 768
    out_ref[0:RANK, :] = (0.5 * total).astype(BF16)
    if top:
        out_ref[RANK:, :] = jnp.zeros((2 * RANK, LANES), BF16)
    else:
        out_ref[RANK:, :] = above_ref[0 : 2 * RANK, :]


def relay(share, above, slope, da, ub):
    first = above is None
    return pl.pallas_call(
        functools.partial(relay_kernel, first),
        out_shape=shaped((3 * RANK, LANES), BF16),
        in_specs=[VMEM] * (8 if first else 9),
        out_specs=VMEM,
        compiler_params=params(14),
        name="relay_first" if first else "relay",
    )(*share, *([] if first else [above]), *slope, da, ub)


def grad_kernel(s0, s1, s2, s3, above_ref, h0, h1, h2, h3, keep_ref, send_ref, grad):
    low = low_of((s0, s1, s2, s3), above_ref).astype(BF16)
    core = core_pos()
    lane = lax.broadcasted_iota(jnp.int32, (RANK, LANES), 1)
    for bucket, hidden_ref in enumerate((h0, h1, h2, h3)):
        grad[...] = jnp.dot(low, hidden_ref[...], preferred_element_type=F32)
        for z in range(ZS):
            for y in range(YS):
                pair = []
                for c in range(2):
                    start = (z * 8 + y * 2 + c) * OWNED
                    base, shift = start // LANES * LANES, start % LANES
                    piece = grad[:, base : base + LANES]
                    if shift:
                        piece = pltpu.roll(piece, LANES - shift, 1)
                    if shift + OWNED > LANES:
                        more = pltpu.roll(
                            grad[:, base + LANES : base + 2 * LANES], LANES - shift, 1
                        )
                        piece = jnp.where(lane < LANES - shift, piece, more)
                    pair.append(piece)
                keep_ref[y, z, bucket] = jnp.where(core == 0, pair[0], pair[1]).astype(BF16)
                send_ref[y, z, bucket] = jnp.where(core == 0, pair[1], pair[0]).astype(BF16)


def grads(share, above, hidden):
    return pl.pallas_call(
        grad_kernel,
        out_shape=[shaped((YS, ZS, BUCKETS, RANK, LANES), BF16)] * 2,
        in_specs=[VMEM] * 9,
        out_specs=[VMEM] * 2,
        scratch_shapes=[pltpu.VMEM((RANK, BUCKET_ROWS), F32)],
        compiler_params=params(14),
        name="grads",
    )(*share, above, *hidden)


def core_sum_kernel(keep_ref, got_ref, own_ref, *outs):
    here = y_pos()
    own_ref[...] = keep_ref[here].astype(F32) + got_ref[here].astype(F32)
    for k, out in enumerate(outs):
        there = lax.rem(here + k + 1, YS)
        out[...] = (keep_ref[there].astype(F32) + got_ref[there].astype(F32)).astype(BF16)


def core_sum(keep, got):
    block = (ZS, BUCKETS, RANK, LANES)
    return pl.pallas_call(
        core_sum_kernel,
        out_shape=[shaped(block, F32)] + [shaped(block, BF16)] * 3,
        in_specs=[VMEM] * 2,
        out_specs=[VMEM] * 4,
        compiler_params=params(),
        name="core_sum",
    )(keep, got)


def y_sum_kernel(own_ref, g1, g2, g3, out_own, *outs):
    here = z_pos()
    for step, out in zip((0, *Z_STEPS), (out_own, *outs)):
        for far in range(2):
            z = here ^ (step ^ (far * Z_PARTNER))
            total = own_ref[z] + g1[z].astype(F32) + g2[z].astype(F32) + g3[z].astype(F32)
            out[far] = total.astype(out.dtype)


def y_sum(own, got):
    block = (2, BUCKETS, RANK, LANES)
    return pl.pallas_call(
        y_sum_kernel,
        out_shape=[shaped(block, F32)] + [shaped(block, BF16)] * 3,
        in_specs=[VMEM] * 4,
        out_specs=[VMEM] * 4,
        compiler_params=params(8),
        name="y_sum",
    )(own, *got)


def z_sum_kernel(own_ref, g1, g2, g3, out_ref):
    total = own_ref[...] + g1[...].astype(F32) + g2[...].astype(F32) + g3[...].astype(F32)
    out_ref[...] = total.astype(BF16)


def z_sum(own, got):
    return pl.pallas_call(
        z_sum_kernel,
        out_shape=shaped((2, BUCKETS, RANK, LANES), BF16),
        in_specs=[VMEM] * 4,
        out_specs=VMEM,
        compiler_params=params(4),
        name="z_sum",
    )(own, *got)


def adamw_kernel(mine_ref, got_ref, own_state, partner_state, weight_out, state_out):
    weight_out[...] = jnp.zeros_like(weight_out)
    for side, state in enumerate((own_state, partner_state)):
        gradient = mine_ref[side].astype(F32) + got_ref[1 - side].astype(F32)
        gradient = gradient[:, :, 0:OWNED]
        weights = state[0]
        first_new = BETA_ONE * state[1] + (1.0 - BETA_ONE) * gradient
        second_new = BETA_TWO * state[2] + (1.0 - BETA_TWO) * gradient * gradient
        first_hat = first_new / (1.0 - BETA_ONE**STEP)
        second_hat = second_new / (1.0 - BETA_TWO**STEP)
        weights_new = weights - LEARN_RATE * (
            first_hat / (jnp.sqrt(second_hat) + EPSILON) + DECAY_RATE * weights
        )
        weight_out[side, :, :, 0:OWNED] = weights_new.astype(BF16)
        if side == 0:
            state_out[0][...] = weights_new
            state_out[1][...] = first_new
            state_out[2][...] = second_new


def adamw(mine, got, state, partner_state):
    block = shaped((BUCKETS, RANK, OWNED), F32)

    def kernel(mine_ref, got_ref, state_ref, partner_ref, weight_out, *state_out):
        adamw_kernel(mine_ref, got_ref, state_ref, partner_ref, weight_out, state_out)

    return pl.pallas_call(
        kernel,
        out_shape=[shaped((2, BUCKETS, RANK, LANES), BF16)] + [block] * 3,
        in_specs=[VMEM] * 4,
        out_specs=[VMEM] * 4,
        compiler_params=params(4),
        name="adamw",
    )(mine, got, state, partner_state)


def assemble_kernel(*refs):
    arrays, (out_ref, blocks, sems) = refs[:8], refs[8:]
    core, y_here, z_here = core_pos(), y_pos(), z_pos()
    copies = []
    for side in range(2):
        for i, k in enumerate(Y_ORDER):
            copies.append(
                pltpu.make_async_copy(
                    arrays[side * YS + i],
                    blocks.at[lax.rem(core + side, 2), lax.rem(y_here + YS - k, YS)],
                    sems.at[side * YS + i],
                )
            )
            copies[-1].start()
    for copy in copies:
        copy.wait()
    lane = lax.broadcasted_iota(jnp.int32, (RANK, LANES), 1)
    places = []
    for z in range(ZS):
        apart = z_here ^ z
        places.append(jnp.where(apart < 4, 2 * apart, 2 * (apart ^ Z_PARTNER) + 1))
    for tile in range(FF // LANES):
        value = None
        first = tile * LANES // OWNED
        last = (tile * LANES + LANES - 1) // OWNED
        for piece in range(first, last + 1):
            bucket, owner = divmod(piece, 64)
            z, y, c = owner // 8, owner // 2 % YS, owner % 2
            block = blocks[c, y, places[z], bucket].astype(F32)
            start = piece * OWNED - tile * LANES
            if start % LANES:
                block = pltpu.roll(block, start % LANES, 1)
            value = block if value is None else jnp.where(lane < start, value, block)
        out_ref[:, tile * LANES : (tile + 1) * LANES] = value.astype(BF16)


def assemble(arrays):
    return pl.pallas_call(
        assemble_kernel,
        out_shape=shaped((RANK, FF), BF16),
        in_specs=[ANY] * 8,
        out_specs=VMEM,
        scratch_shapes=[
            pltpu.VMEM((2, YS, ZS, BUCKETS, RANK, LANES), BF16),
            pltpu.SemaphoreType.DMA((8,)),
        ],
        compiler_params=params(),
        name="assemble",
    )(*arrays)


def per_device(out_grad, pre_act, down_a, down_b, up_a, up_b, master, moment, second):
    da, ub = down_a[0].T, up_b[0].T
    mine = slices(down_b[0], up_a[0].T)
    ws = [mine[0]] + [over_section(mine[k], k) for k in (1, 3, 2)]
    pre = pre_act[0]
    slope = activation(pre, True, 0, 3)
    ws, slope = lax.optimization_barrier((ws, slope))
    share = shares(out_grad, [ws[0], ws[1], ws[3], ws[2]])
    pre, _ = lax.optimization_barrier((pre, share[0]))
    slope = [slope, activation(pre, True, 3)]
    share = [share[0]] + [over_section(share[k], -k) for k in (1, 3, 2)]
    state = jnp.stack([a[0].transpose(0, 2, 1) for a in (master, moment, second)])
    above, hidden = None, []
    for i in range(3):
        sent = relay(share, above, slope, da, ub)
        above = lax.ppermute(sent, "section", [(1, 0), (2, 1), (3, 2)])
        pre, state, _ = lax.optimization_barrier((pre, state, sent))
        if i < 2:
            hidden += [activation(pre, False, 2 * i + b) for b in range(2)]
            above, *hidden = lax.optimization_barrier((above, *hidden))
    partner_state = over_dp(state, zx=Z_PARTNER)
    keep, send = grads(share, above, hidden)
    own, *sends = core_sum(keep, over_dp(send, dc=1))
    own, *sends = y_sum(own, [over_dp(sends[k - 1], dy=k) for k in (1, 3, 2)])
    mine = z_sum(own, [over_dp(a, zx=k) for a, k in zip(sends, Z_STEPS)])
    pair, *state = adamw(mine, over_dp(mine, zx=Z_PARTNER), state, partner_state)
    column = jnp.concatenate([pair] + [over_dp(pair, zx=k) for k in Z_STEPS[::-1]])
    plane = [column] + [over_dp(column, dy=k) for k in Y_ORDER[1:]]
    rows = assemble(plane + [over_dp(a, dc=1) for a in plane])
    return (rows.T[None], *[a.transpose(0, 2, 1)[None] for a in state])


def solution(mesh):
    return jax.shard_map(
        per_device,
        mesh=mesh,
        in_specs=(
            P("dp", "section"),
            P("section", "dp", None),
            P("section", None, None),
            P("section", None, None),
            P("section", None, None),
            P("section", None, None),
            P("section", None, "dp", None),
            P("section", None, "dp", None),
            P("section", None, "dp", None),
        ),
        out_specs=(
            P("section", None, None),
            P("section", None, "dp", None),
            P("section", None, "dp", None),
            P("section", None, "dp", None),
        ),
        check_vma=False,
    )
```

```python
import functools

import jax
import jax.numpy as jnp
from jax import lax
from jax.experimental import pallas as pl
from jax.experimental.pallas import tpu as pltpu
from jax.sharding import PartitionSpec as P

BUCKETS = 4
STEP = 20
BETA_ONE = 0.8
BETA_TWO = 0.95
LEARN_RATE = 0.02
DECAY_RATE = 0.1
EPSILON = 1e-08

TOKENS = 128
FF = 27648
RANK = 32
MODEL = 5120
WIDTH = MODEL // 4
BUCKET_ROWS = FF // BUCKETS
OWNED = 108
LANES = 128
ZS, YS = 8, 4
HALF = ZS // 2
Z_STEPS = (3, 2, 1)
Z_PARTNER = 7
Y_ORDER = (0, 2, 3, 1)
BF16, F32 = jnp.bfloat16, jnp.float32
VMEM = pl.BlockSpec(memory_space=pltpu.VMEM)
ANY = pl.BlockSpec(memory_space=pl.ANY)
HBM = pl.BlockSpec(memory_space=pltpu.HBM)
CONTRACT_LAST = (((1,), (1,)), ((), ()))


def params(mib=16):
    return pltpu.CompilerParams(vmem_limit_bytes=mib * 1024 * 1024)


def in_hbm(array):
    return pltpu.with_memory_space_constraint(array, pltpu.HBM)


def shaped(shape, dtype):
    return jax.ShapeDtypeStruct(shape, dtype)


def z_pos():
    return lax.axis_index("dp") // 8


def y_pos():
    return (lax.axis_index("dp") // 2) % YS


def core_pos():
    return lax.axis_index("dp") % 2


def over_dp(value, zx=0, dy=0, dc=0):
    pairs = []
    for z in range(ZS):
        for y in range(YS):
            for c in range(2):
                target = (z ^ zx) * 8 + ((y + dy) % YS) * 2 + (c + dc) % 2
                pairs.append((z * 8 + y * 2 + c, target))
    return lax.ppermute(value, "dp", pairs)


def over_section(value, steps):
    return lax.ppermute(value, "section", [(i, (i + steps) % 4) for i in range(4)])


def slice_kernel(db_ref, ua_ref, *refs):
    outs, sems = refs[:4], refs[4]
    here = lax.axis_index("section")
    copies = []
    for k, out in enumerate(outs):
        columns = pl.ds(pl.multiple_of(lax.rem(here + k, 4) * WIDTH, LANES), WIDTH)
        for i, ref in enumerate((db_ref, ua_ref)):
            copies.append(
                pltpu.make_async_copy(
                    ref.at[:, columns], out.at[pl.ds(i * RANK, RANK), :], sems.at[2 * k + i]
                )
            )
            copies[-1].start()
    for copy in copies:
        copy.wait()


def slices(db, ua):
    return pl.pallas_call(
        slice_kernel,
        out_shape=[shaped((2 * RANK, WIDTH), BF16)] * 4,
        in_specs=[HBM] * 2,
        out_specs=[VMEM] * 4,
        scratch_shapes=[pltpu.SemaphoreType.DMA((8,))],
        compiler_params=params(4),
        name="slices",
    )(in_hbm(db), in_hbm(ua))


def activation_kernel(slope, first, parts, pre_ref, out_ref, held, sems):
    size = held.shape[1] // parts
    copies = []
    for i in range(parts):
        copies.append(
            pltpu.make_async_copy(
                pre_ref.at[:, pl.ds(first + i * size, size)],
                held.at[:, pl.ds(i * size, size)],
                sems.at[i],
            )
        )
        copies[-1].start()

    def chunk(i, _):
        columns = pl.ds(pl.multiple_of(i * 256, 256), 256)
        for row in range(0, TOKENS, 32):
            rows = slice(row, row + 32)
            half = 0.5 * held[rows, columns].astype(F32)
            t = jnp.tanh(half)
            value = (1.0 + t) * (1.0 + half * (1.0 - t)) if slope else half + half * t
            out_ref[rows, columns] = value.astype(BF16)
        return 0

    for i, copy in enumerate(copies):
        copy.wait()
        lax.fori_loop(i * size // 256, (i + 1) * size // 256, chunk, 0)


def activation(pre, slope, bucket, count=1):
    width, parts = BUCKET_ROWS * count, 3 * count
    return pl.pallas_call(
        functools.partial(activation_kernel, slope, bucket * BUCKET_ROWS, parts),
        out_shape=shaped((TOKENS, width), BF16),
        in_specs=[HBM],
        out_specs=VMEM,
        scratch_shapes=[
            pltpu.VMEM((TOKENS, width), BF16),
            pltpu.SemaphoreType.DMA((parts,)),
        ],
        compiler_params=params(4 * count + 2),
        cost_estimate=pl.CostEstimate(
            flops=10 * TOKENS * width,
            bytes_accessed=4 * TOKENS * width,
            transcendentals=TOKENS * width,
        ),
        name="slope" if slope else "hidden",
    )(in_hbm(pre))


def share_kernel(g_ref, w0, w1, w2, w3, *outs):
    ws = (w0, w1, w2, w3)
    for k, out in enumerate(outs):
        db = ws[k][0:RANK, :]
        out[:, 0:LANES] = lax.dot_general(
            db, g_ref[...], CONTRACT_LAST, preferred_element_type=F32
        )
        rows = jnp.concatenate([ws[(k - m) % 4][RANK:, :] for m in (1, 2, 3, 0)], axis=0)
        out[:, LANES:] = lax.dot_general(db, rows, CONTRACT_LAST, preferred_element_type=F32)


def shares(g, ws):
    return pl.pallas_call(
        share_kernel,
        out_shape=[shaped((RANK, 2 * LANES), F32)] * 4,
        in_specs=[VMEM] * 5,
        out_specs=[VMEM] * 4,
        compiler_params=params(),
        name="shares",
    )(g, *ws)


def low_of(share_refs, above_ref):
    total = share_refs[0][...] + share_refs[1][...] + share_refs[2][...] + share_refs[3][...]
    low = total[:, 0:LANES]
    if above_ref is not None:
        low = low + jnp.dot(
            total[:, LANES : LANES + 3 * RANK],
            above_ref[...].astype(F32),
            preferred_element_type=F32,
            precision=lax.Precision.HIGHEST,
        )
    return low


def relay_kernel(top, *refs):
    share_refs, refs = refs[:4], refs[4:]
    above_ref = None
    if not top:
        above_ref, refs = refs[0], refs[1:]
    slope_ref, da_ref, ub_ref, out_ref = refs
    low = low_of(share_refs, above_ref).T.astype(BF16)
    total = jnp.zeros((RANK, TOKENS), F32)

    for start in range(0, FF, 768):
        columns = slice(start, start + 768)
        upstream = jnp.dot(low, da_ref[:, columns], preferred_element_type=F32)
        delta = (upstream * slope_ref[:, columns].astype(F32)).astype(BF16)
        total = total + lax.dot_general(
            ub_ref[:, columns], delta, CONTRACT_LAST, preferred_element_type=F32
        )
    out_ref[0:RANK, :] = (0.5 * total).astype(BF16)
    if top:
        out_ref[RANK:, :] = jnp.zeros((2 * RANK, LANES), BF16)
    else:
        out_ref[RANK:, :] = above_ref[0 : 2 * RANK, :]


def relay(share, above, slope, da, ub):
    first = above is None
    return pl.pallas_call(
        functools.partial(relay_kernel, first),
        out_shape=shaped((3 * RANK, LANES), BF16),
        in_specs=[VMEM] * (7 if first else 8),
        out_specs=VMEM,
        compiler_params=params(14),
        name="relay_first" if first else "relay",
    )(*share, *([] if first else [above]), slope, da, ub)


def grad_kernel(s0, s1, s2, s3, above_ref, h0, h1, h2, h3, keep_ref, send_ref, grad):
    low = low_of((s0, s1, s2, s3), above_ref).astype(BF16)
    core = core_pos()
    lane = lax.broadcasted_iota(jnp.int32, (RANK, LANES), 1)
    for bucket, hidden_ref in enumerate((h0, h1, h2, h3)):
        grad[...] = jnp.dot(low, hidden_ref[...], preferred_element_type=F32)
        for z in range(ZS):
            for y in range(YS):
                pair = []
                for c in range(2):
                    start = (z * 8 + y * 2 + c) * OWNED
                    base, shift = start // LANES * LANES, start % LANES
                    piece = grad[:, base : base + LANES]
                    if shift:
                        piece = pltpu.roll(piece, LANES - shift, 1)
                    if shift + OWNED > LANES:
                        more = pltpu.roll(
                            grad[:, base + LANES : base + 2 * LANES], LANES - shift, 1
                        )
                        piece = jnp.where(lane < LANES - shift, piece, more)
                    pair.append(piece)
                keep_ref[y, z, bucket] = jnp.where(core == 0, pair[0], pair[1]).astype(BF16)
                send_ref[y, z, bucket] = jnp.where(core == 0, pair[1], pair[0]).astype(BF16)


def grads(share, above, hidden):
    return pl.pallas_call(
        grad_kernel,
        out_shape=[shaped((YS, ZS, BUCKETS, RANK, LANES), BF16)] * 2,
        in_specs=[VMEM] * 9,
        out_specs=[VMEM] * 2,
        scratch_shapes=[pltpu.VMEM((RANK, BUCKET_ROWS), F32)],
        compiler_params=params(14),
        name="grads",
    )(*share, above, *hidden)


def core_sum_kernel(keep_ref, got_ref, own_ref, up_ref, down_ref, up_held, down_held):
    here = y_pos()
    first, second = slice(0, HALF), slice(HALF, ZS)

    def block(ahead, half):
        y = lax.rem(here + ahead, YS)
        return keep_ref[y, half].astype(F32) + got_ref[y, half].astype(F32)

    own_ref[first] = block(0, first)
    own_ref[second] = block(0, second)
    up_ref[0] = block(2, first).astype(BF16)
    up_ref[1] = block(1, second).astype(BF16)
    down_ref[0] = block(2, second).astype(BF16)
    down_ref[1] = block(3, first).astype(BF16)
    up_held[...] = block(1, first)
    down_held[...] = block(3, second)


def core_sum(keep, got):
    half = (HALF, BUCKETS, RANK, LANES)
    return pl.pallas_call(
        core_sum_kernel,
        out_shape=[shaped((ZS, BUCKETS, RANK, LANES), F32)]
        + [shaped((2, *half), BF16)] * 2
        + [shaped(half, F32)] * 2,
        in_specs=[VMEM] * 2,
        out_specs=[VMEM] * 5,
        compiler_params=params(8),
        name="core_sum",
    )(keep, got)


def y_pass_kernel(up_held, from_below, down_held, from_above, up_ref, down_ref):
    up_ref[...] = (up_held[...] + from_below[0].astype(F32)).astype(BF16)
    down_ref[...] = (down_held[...] + from_above[0].astype(F32)).astype(BF16)


def y_pass(up_held, from_below, down_held, from_above):
    return pl.pallas_call(
        y_pass_kernel,
        out_shape=[shaped((HALF, BUCKETS, RANK, LANES), BF16)] * 2,
        in_specs=[VMEM] * 4,
        out_specs=[VMEM] * 2,
        compiler_params=params(4),
        name="y_pass",
    )(up_held, from_below, down_held, from_above)


def y_sum_kernel(own_ref, from_below, from_above, last_below, last_above, out_own, *outs):
    here = z_pos()
    for step, out in zip((0, *Z_STEPS), (out_own, *outs)):
        for far in range(2):
            z = here ^ (step ^ (far * Z_PARTNER))
            place = z & (HALF - 1)
            first = from_above[1, place].astype(F32) + last_below[place].astype(F32)
            second = from_below[1, place].astype(F32) + last_above[place].astype(F32)
            total = own_ref[z] + jnp.where(z < HALF, first, second)
            out[far] = total.astype(out.dtype)


def y_sum(*terms):
    block = (2, BUCKETS, RANK, LANES)
    return pl.pallas_call(
        y_sum_kernel,
        out_shape=[shaped(block, F32)] + [shaped(block, BF16)] * 3,
        in_specs=[VMEM] * 5,
        out_specs=[VMEM] * 4,
        compiler_params=params(8),
        name="y_sum",
    )(*terms)


def z_sum_kernel(own_ref, g1, g2, g3, out_ref):
    total = own_ref[...] + g1[...].astype(F32) + g2[...].astype(F32) + g3[...].astype(F32)
    out_ref[...] = total.astype(BF16)


def z_sum(own, got):
    return pl.pallas_call(
        z_sum_kernel,
        out_shape=shaped((2, BUCKETS, RANK, LANES), BF16),
        in_specs=[VMEM] * 4,
        out_specs=VMEM,
        compiler_params=params(4),
        name="z_sum",
    )(own, *got)


def adamw_kernel(mine_ref, got_ref, own_state, partner_state, weight_out, state_out):
    weight_out[...] = jnp.zeros_like(weight_out)
    for side, state in enumerate((own_state, partner_state)):
        gradient = mine_ref[side].astype(F32) + got_ref[1 - side].astype(F32)
        gradient = gradient[:, :, 0:OWNED]
        weights = state[0]
        first_new = BETA_ONE * state[1] + (1.0 - BETA_ONE) * gradient
        second_new = BETA_TWO * state[2] + (1.0 - BETA_TWO) * gradient * gradient
        first_hat = first_new / (1.0 - BETA_ONE**STEP)
        second_hat = second_new / (1.0 - BETA_TWO**STEP)
        weights_new = weights - LEARN_RATE * (
            first_hat / (jnp.sqrt(second_hat) + EPSILON) + DECAY_RATE * weights
        )
        weight_out[side, :, :, 0:OWNED] = weights_new.astype(BF16)
        if side == 0:
            state_out[0][...] = weights_new
            state_out[1][...] = first_new
            state_out[2][...] = second_new


def adamw(mine, got, state, partner_state):
    block = shaped((BUCKETS, RANK, OWNED), F32)

    def kernel(mine_ref, got_ref, state_ref, partner_ref, weight_out, *state_out):
        adamw_kernel(mine_ref, got_ref, state_ref, partner_ref, weight_out, state_out)

    return pl.pallas_call(
        kernel,
        out_shape=[shaped((2, BUCKETS, RANK, LANES), BF16)] + [block] * 3,
        in_specs=[VMEM] * 4,
        out_specs=[VMEM] * 4,
        compiler_params=params(4),
        name="adamw",
    )(mine, got, state, partner_state)


def assemble_kernel(*refs):
    arrays, (out_ref, blocks, sems) = refs[:8], refs[8:]
    core, y_here, z_here = core_pos(), y_pos(), z_pos()
    copies = []
    for side in range(2):
        for i, k in enumerate(Y_ORDER):
            copies.append(
                pltpu.make_async_copy(
                    arrays[side * YS + i],
                    blocks.at[lax.rem(core + side, 2), lax.rem(y_here + YS - k, YS)],
                    sems.at[side * YS + i],
                )
            )
            copies[-1].start()
    for copy in copies:
        copy.wait()
    lane = lax.broadcasted_iota(jnp.int32, (RANK, LANES), 1)
    places = []
    for z in range(ZS):
        apart = z_here ^ z
        places.append(jnp.where(apart < 4, 2 * apart, 2 * (apart ^ Z_PARTNER) + 1))
    for tile in range(FF // LANES):
        value = None
        first = tile * LANES // OWNED
        last = (tile * LANES + LANES - 1) // OWNED
        for piece in range(first, last + 1):
            bucket, owner = divmod(piece, 64)
            z, y, c = owner // 8, owner // 2 % YS, owner % 2
            block = blocks[c, y, places[z], bucket].astype(F32)
            start = piece * OWNED - tile * LANES
            if start % LANES:
                block = pltpu.roll(block, start % LANES, 1)
            value = block if value is None else jnp.where(lane < start, value, block)
        out_ref[:, tile * LANES : (tile + 1) * LANES] = value.astype(BF16)


def assemble(arrays):
    return pl.pallas_call(
        assemble_kernel,
        out_shape=shaped((RANK, FF), BF16),
        in_specs=[ANY] * 8,
        out_specs=VMEM,
        scratch_shapes=[
            pltpu.VMEM((2, YS, ZS, BUCKETS, RANK, LANES), BF16),
            pltpu.SemaphoreType.DMA((8,)),
        ],
        compiler_params=params(),
        name="assemble",
    )(*arrays)


def per_device(out_grad, pre_act, down_a, down_b, up_a, up_b, master, moment, second):
    da, ub = down_a[0].T, up_b[0].T
    mine = slices(down_b[0], up_a[0].T)
    ws = [mine[0]] + [over_section(mine[k], k) for k in (1, 3, 2)]
    pre = pre_act[0]
    slope = activation(pre, True, 0, BUCKETS)
    ws, slope = lax.optimization_barrier((ws, slope))
    share = shares(out_grad, [ws[0], ws[1], ws[3], ws[2]])
    pre, _ = lax.optimization_barrier((pre, share[0]))
    hidden = [activation(pre, False, 0)]
    share = [share[0]] + [over_section(share[k], -k) for k in (1, 3, 2)]
    state = jnp.stack([a[0].transpose(0, 2, 1) for a in (master, moment, second)])
    *share, first_hidden = lax.optimization_barrier((*share, hidden[0]))
    above, hidden = None, [first_hidden]
    for buckets in ((1, 2), (3,), ()):
        sent = relay(share, above, slope, da, ub)
        above = lax.ppermute(sent, "section", [(1, 0), (2, 1), (3, 2)])
        if buckets:
            pre, _ = lax.optimization_barrier((pre, sent))
            hidden += [activation(pre, False, b) for b in buckets]
            above, state, *hidden = lax.optimization_barrier((above, state, *hidden))
    keep, send = grads(share, above, hidden)
    own, up, down, up_held, down_held = core_sum(keep, over_dp(send, dc=1))
    state, own = lax.optimization_barrier((state, own))
    partner_state = over_dp(state, zx=Z_PARTNER)
    from_below, from_above = over_dp(up, dy=1), over_dp(down, dy=-1)
    up, down = y_pass(up_held, from_below, down_held, from_above)
    last_below, last_above = over_dp(up, dy=1), over_dp(down, dy=-1)
    last_below, partner_state = lax.optimization_barrier((last_below, partner_state))
    own, *sends = y_sum(own, from_below, from_above, last_below, last_above)
    mine = z_sum(own, [over_dp(a, zx=k) for a, k in zip(sends, Z_STEPS)])
    pair, *state = adamw(mine, over_dp(mine, zx=Z_PARTNER), state, partner_state)
    column = jnp.concatenate([pair] + [over_dp(pair, zx=k) for k in Z_STEPS[::-1]])
    plane = [column] + [over_dp(column, dy=k) for k in Y_ORDER[1:]]
    rows = assemble(plane + [over_dp(a, dc=1) for a in plane])
    return (rows.T[None], *[a.transpose(0, 2, 1)[None] for a in state])


def solution(mesh):
    return jax.shard_map(
        per_device,
        mesh=mesh,
        in_specs=(
            P("dp", "section"),
            P("section", "dp", None),
            P("section", None, None),
            P("section", None, None),
            P("section", None, None),
            P("section", None, None),
            P("section", None, "dp", None),
            P("section", None, "dp", None),
            P("section", None, "dp", None),
        ),
        out_specs=(
            P("section", None, None),
            P("section", None, "dp", None),
            P("section", None, "dp", None),
            P("section", None, "dp", None),
        ),
        check_vma=False,
    )
```

```python
import functools

import jax
import jax.numpy as jnp
from jax import lax
from jax.experimental import pallas as pl
from jax.experimental.pallas import tpu as pltpu
from jax.sharding import PartitionSpec as P

BUCKETS = 4
STEP = 20
BETA_ONE = 0.8
BETA_TWO = 0.95
LEARN_RATE = 0.02
DECAY_RATE = 0.1
EPSILON = 1e-08

TOKENS = 128
FF = 27648
RANK = 32
MODEL = 5120
WIDTH = MODEL // 4
BUCKET_ROWS = FF // BUCKETS
OWNED = 108
LANES = 128
ZS, YS = 8, 4
HALF = ZS // 2
Z_STEPS = (3, 2, 1)
Z_PARTNER = 7
Y_ORDER = (0, 1, 3, 2)
BF16, F32 = jnp.bfloat16, jnp.float32
VMEM = pl.BlockSpec(memory_space=pltpu.VMEM)
ANY = pl.BlockSpec(memory_space=pl.ANY)
HBM = pl.BlockSpec(memory_space=pltpu.HBM)
CONTRACT_LAST = (((1,), (1,)), ((), ()))


def params(mib=16):
    return pltpu.CompilerParams(vmem_limit_bytes=mib * 1024 * 1024)


def in_hbm(array):
    return pltpu.with_memory_space_constraint(array, pltpu.HBM)


def shaped(shape, dtype):
    return jax.ShapeDtypeStruct(shape, dtype)


def z_pos():
    return lax.axis_index("dp") >> 3


def y_pos():
    return (lax.axis_index("dp") >> 1) & (YS - 1)


def core_pos():
    return lax.axis_index("dp") & 1


def over_dp(value, zx=0, dy=0, dc=0):
    pairs = []
    for z in range(ZS):
        for y in range(YS):
            for c in range(2):
                target = (z ^ zx) * 8 + ((y + dy) % YS) * 2 + (c + dc) % 2
                pairs.append((z * 8 + y * 2 + c, target))
    return lax.ppermute(value, "dp", pairs)


def over_section(value, steps):
    return lax.ppermute(value, "section", [(i, (i + steps) % 4) for i in range(4)])


def slice_kernel(db_ref, ua_ref, *refs):
    outs, sems = refs[:4], refs[4]
    here = lax.axis_index("section")
    copies = []
    for k, out in enumerate(outs):
        columns = pl.ds(pl.multiple_of(lax.rem(here + k, 4) * WIDTH, LANES), WIDTH)
        for i, ref in enumerate((db_ref, ua_ref)):
            copies.append(
                pltpu.make_async_copy(
                    ref.at[:, columns], out.at[pl.ds(i * RANK, RANK), :], sems.at[2 * k + i]
                )
            )
            copies[-1].start()
    for copy in copies:
        copy.wait()


def slices(db, ua):
    return pl.pallas_call(
        slice_kernel,
        out_shape=[shaped((2 * RANK, WIDTH), BF16)] * 4,
        in_specs=[HBM] * 2,
        out_specs=[VMEM] * 4,
        scratch_shapes=[pltpu.SemaphoreType.DMA((8,))],
        compiler_params=params(4),
        name="slices",
    )(in_hbm(db), in_hbm(ua))


def activation_kernel(slope, first, parts, pre_ref, out_ref, held, sems):
    size = held.shape[1] // parts
    copies = []
    for i in range(parts):
        copies.append(
            pltpu.make_async_copy(
                pre_ref.at[:, pl.ds(first + i * size, size)],
                held.at[:, pl.ds(i * size, size)],
                sems.at[i],
            )
        )
        copies[-1].start()

    def chunk(i, _):
        columns = pl.ds(pl.multiple_of(i * 256, 256), 256)
        for row in range(0, TOKENS, 32):
            rows = slice(row, row + 32)
            half = 0.5 * held[rows, columns].astype(F32)
            t = jnp.tanh(half)
            value = (1.0 + t) * (1.0 + half * (1.0 - t)) if slope else half + half * t
            out_ref[rows, columns] = value.astype(BF16)
        return 0

    for i, copy in enumerate(copies):
        copy.wait()
        lax.fori_loop(i * size // 256, (i + 1) * size // 256, chunk, 0)


def activation(pre, slope, bucket, count=1):
    width, parts = BUCKET_ROWS * count, 3 * count
    return pl.pallas_call(
        functools.partial(activation_kernel, slope, bucket * BUCKET_ROWS, parts),
        out_shape=shaped((TOKENS, width), BF16),
        in_specs=[HBM],
        out_specs=VMEM,
        scratch_shapes=[
            pltpu.VMEM((TOKENS, width), BF16),
            pltpu.SemaphoreType.DMA((parts,)),
        ],
        compiler_params=params(4 * count + 2),
        cost_estimate=pl.CostEstimate(
            flops=10 * TOKENS * width,
            bytes_accessed=4 * TOKENS * width,
            transcendentals=TOKENS * width,
        ),
        name="slope" if slope else "hidden",
    )(in_hbm(pre))


def share_kernel(g_ref, w0, w1, w2, w3, *outs):
    ws = (w0, w1, w2, w3)
    for k, out in enumerate(outs):
        db = ws[k][0:RANK, :]
        out[:, 0:LANES] = lax.dot_general(
            db, g_ref[...], CONTRACT_LAST, preferred_element_type=F32
        )
        rows = jnp.concatenate([ws[(k - m) % 4][RANK:, :] for m in (1, 2, 3, 0)], axis=0)
        out[:, LANES:] = lax.dot_general(db, rows, CONTRACT_LAST, preferred_element_type=F32)


def shares(g, ws):
    return pl.pallas_call(
        share_kernel,
        out_shape=[shaped((RANK, 2 * LANES), F32)] * 4,
        in_specs=[VMEM] * 5,
        out_specs=[VMEM] * 4,
        compiler_params=params(),
        name="shares",
    )(g, *ws)


def low_of(share_refs, above_ref):
    total = share_refs[0][...] + share_refs[1][...] + share_refs[2][...] + share_refs[3][...]
    low = total[:, 0:LANES]
    if above_ref is not None:
        low = low + jnp.dot(
            total[:, LANES : LANES + 3 * RANK],
            above_ref[...].astype(F32),
            preferred_element_type=F32,
            precision=lax.Precision.HIGHEST,
        )
    return low


def relay_kernel(top, *refs):
    share_refs, refs = refs[:4], refs[4:]
    above_ref = None
    if not top:
        above_ref, refs = refs[0], refs[1:]
    slope_ref, da_ref, ub_ref, out_ref = refs
    low = low_of(share_refs, above_ref).T.astype(BF16)
    total = jnp.zeros((RANK, TOKENS), F32)

    for start in range(0, FF, 768):
        columns = slice(start, start + 768)
        upstream = jnp.dot(low, da_ref[:, columns], preferred_element_type=F32)
        delta = (upstream * slope_ref[:, columns].astype(F32)).astype(BF16)
        total = total + lax.dot_general(
            ub_ref[:, columns], delta, CONTRACT_LAST, preferred_element_type=F32
        )
    out_ref[0:RANK, :] = (0.5 * total).astype(BF16)
    if top:
        out_ref[RANK:, :] = jnp.zeros((2 * RANK, LANES), BF16)
    else:
        out_ref[RANK:, :] = above_ref[0 : 2 * RANK, :]


def relay(share, above, slope, da, ub):
    first = above is None
    return pl.pallas_call(
        functools.partial(relay_kernel, first),
        out_shape=shaped((3 * RANK, LANES), BF16),
        in_specs=[VMEM] * (7 if first else 8),
        out_specs=VMEM,
        compiler_params=params(14),
        name="relay_first" if first else "relay",
    )(*share, *([] if first else [above]), slope, da, ub)


def grad_kernel(s0, s1, s2, s3, above_ref, h0, h1, h2, h3, keep_ref, send_ref, grad):
    low = low_of((s0, s1, s2, s3), above_ref).astype(BF16)
    core = core_pos()
    lane = lax.broadcasted_iota(jnp.int32, (RANK, LANES), 1)
    for bucket, hidden_ref in enumerate((h0, h1, h2, h3)):
        grad[...] = jnp.dot(low, hidden_ref[...], preferred_element_type=F32)
        for z in range(ZS):
            for y in range(YS):
                pair = []
                for c in range(2):
                    start = (z * 8 + y * 2 + c) * OWNED
                    base, shift = start // LANES * LANES, start % LANES
                    piece = grad[:, base : base + LANES]
                    if shift:
                        piece = pltpu.roll(piece, LANES - shift, 1)
                    if shift + OWNED > LANES:
                        more = pltpu.roll(
                            grad[:, base + LANES : base + 2 * LANES], LANES - shift, 1
                        )
                        piece = jnp.where(lane < LANES - shift, piece, more)
                    pair.append(piece)
                keep_ref[y, z, bucket] = jnp.where(core == 0, pair[0], pair[1]).astype(BF16)
                send_ref[y, z, bucket] = jnp.where(core == 0, pair[1], pair[0]).astype(BF16)


def grads(share, above, hidden):
    return pl.pallas_call(
        grad_kernel,
        out_shape=[shaped((YS, ZS, BUCKETS, RANK, LANES), BF16)] * 2,
        in_specs=[VMEM] * 9,
        out_specs=[VMEM] * 2,
        scratch_shapes=[pltpu.VMEM((RANK, BUCKET_ROWS), F32)],
        compiler_params=params(14),
        name="grads",
    )(*share, above, *hidden)


def core_sum_kernel(keep_ref, got_ref, own_ref, up_ref, down_ref, up_held, down_held):
    here = y_pos()
    first, second = slice(0, HALF), slice(HALF, ZS)

    def block(ahead, half):
        y = lax.rem(here + ahead, YS)
        return keep_ref[y, half].astype(F32) + got_ref[y, half].astype(F32)

    own_ref[first] = block(0, first)
    own_ref[second] = block(0, second)
    up_ref[0] = block(2, first).astype(BF16)
    up_ref[1] = block(1, second).astype(BF16)
    down_ref[0] = block(2, second).astype(BF16)
    down_ref[1] = block(3, first).astype(BF16)
    up_held[...] = block(1, first)
    down_held[...] = block(3, second)


def core_sum(keep, got):
    half = (HALF, BUCKETS, RANK, LANES)
    return pl.pallas_call(
        core_sum_kernel,
        out_shape=[shaped((ZS, BUCKETS, RANK, LANES), F32)]
        + [shaped((2, *half), BF16)] * 2
        + [shaped(half, F32)] * 2,
        in_specs=[VMEM] * 2,
        out_specs=[VMEM] * 5,
        compiler_params=params(8),
        name="core_sum",
    )(keep, got)


def y_pass_kernel(up_held, from_below, down_held, from_above, up_ref, down_ref):
    up_ref[...] = (up_held[...] + from_below[0].astype(F32)).astype(BF16)
    down_ref[...] = (down_held[...] + from_above[0].astype(F32)).astype(BF16)


def y_pass(up_held, from_below, down_held, from_above):
    return pl.pallas_call(
        y_pass_kernel,
        out_shape=[shaped((HALF, BUCKETS, RANK, LANES), BF16)] * 2,
        in_specs=[VMEM] * 4,
        out_specs=[VMEM] * 2,
        compiler_params=params(4),
        name="y_pass",
    )(up_held, from_below, down_held, from_above)


def y_sum_kernel(own_ref, from_below, from_above, last_below, last_above, out_own, *outs):
    here = z_pos()
    for step, out in zip((0, *Z_STEPS), (out_own, *outs)):
        for far in range(2):
            z = here ^ (step ^ (far * Z_PARTNER))
            place = z & (HALF - 1)
            first = from_above[1, place].astype(F32) + last_below[place].astype(F32)
            second = from_below[1, place].astype(F32) + last_above[place].astype(F32)
            total = own_ref[z] + jnp.where(z < HALF, first, second)
            out[far] = total.astype(out.dtype)


def y_sum(*terms):
    block = (2, BUCKETS, RANK, LANES)
    return pl.pallas_call(
        y_sum_kernel,
        out_shape=[shaped(block, F32)] + [shaped(block, BF16)] * 3,
        in_specs=[VMEM] * 5,
        out_specs=[VMEM] * 4,
        compiler_params=params(8),
        name="y_sum",
    )(*terms)


def z_sum_kernel(own_ref, g1, g2, g3, out_ref):
    total = own_ref[...] + g1[...].astype(F32) + g2[...].astype(F32) + g3[...].astype(F32)
    out_ref[...] = total.astype(BF16)


def z_sum(own, got):
    return pl.pallas_call(
        z_sum_kernel,
        out_shape=shaped((2, BUCKETS, RANK, LANES), BF16),
        in_specs=[VMEM] * 4,
        out_specs=VMEM,
        compiler_params=params(4),
        name="z_sum",
    )(own, *got)


def adamw_kernel(mine_ref, got_ref, own_state, partner_state, weight_out, state_out):
    weight_out[...] = jnp.zeros_like(weight_out)
    for side, state in enumerate((own_state, partner_state)):
        gradient = mine_ref[side].astype(F32) + got_ref[1 - side].astype(F32)
        gradient = gradient[:, :, 0:OWNED]
        weights = state[0]
        first_new = BETA_ONE * state[1] + (1.0 - BETA_ONE) * gradient
        second_new = BETA_TWO * state[2] + (1.0 - BETA_TWO) * gradient * gradient
        first_hat = first_new / (1.0 - BETA_ONE**STEP)
        second_hat = second_new / (1.0 - BETA_TWO**STEP)
        weights_new = weights - LEARN_RATE * (
            first_hat / (jnp.sqrt(second_hat) + EPSILON) + DECAY_RATE * weights
        )
        weight_out[side, :, :, 0:OWNED] = weights_new.astype(BF16)
        if side == 0:
            state_out[0][...] = weights_new
            state_out[1][...] = first_new
            state_out[2][...] = second_new


def adamw(mine, got, state, partner_state):
    block = shaped((BUCKETS, RANK, OWNED), F32)

    def kernel(mine_ref, got_ref, state_ref, partner_ref, weight_out, *state_out):
        adamw_kernel(mine_ref, got_ref, state_ref, partner_ref, weight_out, state_out)

    return pl.pallas_call(
        kernel,
        out_shape=[shaped((2, BUCKETS, RANK, LANES), BF16)] + [block] * 3,
        in_specs=[VMEM] * 4,
        out_specs=[VMEM] * 4,
        compiler_params=params(4),
        name="adamw",
    )(mine, got, state, partner_state)


def assemble_kernel(blocks, out_ref):
    z_here = z_pos()
    lane = lax.broadcasted_iota(jnp.int32, (RANK, LANES), 1)
    places = []
    for z in range(ZS):
        apart = z_here ^ z
        far = jnp.where(apart < HALF, 0, 1)
        step = apart ^ (far * Z_PARTNER)
        places.append(2 * ((HALF - step) & (HALF - 1)) + far)
    for tile in range(FF // LANES):
        value = None
        first = tile * LANES // OWNED
        last = (tile * LANES + LANES - 1) // OWNED
        for piece in range(first, last + 1):
            bucket, owner = divmod(piece, 64)
            z, y, c = owner // 8, owner // 2 % YS, owner % 2
            block = blocks[c, y, places[z], bucket].astype(F32)
            start = piece * OWNED - tile * LANES
            if start % LANES:
                block = pltpu.roll(block, start % LANES, 1)
            value = block if value is None else jnp.where(lane < start, value, block)
        out_ref[:, tile * LANES : (tile + 1) * LANES] = value.astype(BF16)


def assemble(blocks):
    return pl.pallas_call(
        assemble_kernel,
        out_shape=shaped((RANK, FF), BF16),
        in_specs=[VMEM],
        out_specs=VMEM,
        compiler_params=params(8),
        name="assemble",
    )(blocks)


def per_device(out_grad, pre_act, down_a, down_b, up_a, up_b, master, moment, second):
    da, ub = down_a[0].T, up_b[0].T
    mine = slices(down_b[0], up_a[0].T)
    ws = [mine[0]] + [over_section(mine[k], k) for k in (1, 3, 2)]
    pre = pre_act[0]
    slope = activation(pre, True, 0, BUCKETS)
    ws, slope = lax.optimization_barrier((ws, slope))
    share = shares(out_grad, [ws[0], ws[1], ws[3], ws[2]])
    pre, _ = lax.optimization_barrier((pre, share[0]))
    hidden = [activation(pre, False, 0)]
    share = [share[0]] + [over_section(share[k], -k) for k in (1, 3, 2)]
    state = jnp.stack([a[0].transpose(0, 2, 1) for a in (master, moment, second)])
    *share, first_hidden = lax.optimization_barrier((*share, hidden[0]))
    above, hidden = None, [first_hidden]
    for buckets in ((1,), (2, 3), ()):
        sent = relay(share, above, slope, da, ub)
        above = lax.ppermute(sent, "section", [(1, 0), (2, 1), (3, 2)])
        if buckets:
            pre, _ = lax.optimization_barrier((pre, sent))
            hidden += [activation(pre, False, b) for b in buckets]
            above, state, *hidden = lax.optimization_barrier((above, state, *hidden))
    keep, send = grads(share, above, hidden)
    own, up, down, up_held, down_held = core_sum(keep, over_dp(send, dc=1))
    state, own = lax.optimization_barrier((state, own))
    partner_state = over_dp(state, zx=Z_PARTNER)
    from_below, from_above = over_dp(up, dy=1), over_dp(down, dy=-1)
    up, down = y_pass(up_held, from_below, down_held, from_above)
    last_below, last_above = over_dp(up, dy=1), over_dp(down, dy=-1)
    own, *sends = y_sum(own, from_below, from_above, last_below, last_above)
    got = [over_dp(a, zx=k) for a, k in zip(sends, Z_STEPS)]
    *got, partner_state = lax.optimization_barrier((*got, partner_state))
    mine = z_sum(own, got)
    pair, *state = adamw(mine, over_dp(mine, zx=Z_PARTNER), state, partner_state)
    column = jnp.concatenate([pair] + [over_dp(pair, zx=k) for k in Z_STEPS])
    plane = [column] + [over_dp(column, dy=k) for k in Y_ORDER[1:]]
    plane += [over_dp(a, dc=1) for a in plane]
    blocks = jnp.zeros((2, YS, *column.shape), BF16)
    for i, array in enumerate(plane):
        core, y = core_pos() ^ (i // YS), (y_pos() + YS - Y_ORDER[i % YS]) & (YS - 1)
        blocks = lax.dynamic_update_slice(blocks, array[None, None], (core, y, 0, 0, 0, 0))
    rows = assemble(blocks)
    return (rows.T[None], *[a.transpose(0, 2, 1)[None] for a in state])


def solution(mesh):
    return jax.shard_map(
        per_device,
        mesh=mesh,
        in_specs=(
            P("dp", "section"),
            P("section", "dp", None),
            P("section", None, None),
            P("section", None, None),
            P("section", None, None),
            P("section", None, None),
            P("section", None, "dp", None),
            P("section", None, "dp", None),
            P("section", None, "dp", None),
        ),
        out_specs=(
            P("section", None, None),
            P("section", None, "dp", None),
            P("section", None, "dp", None),
            P("section", None, "dp", None),
        ),
        check_vma=False,
    )
```

```python
import functools

import jax
import jax.numpy as jnp
from jax import lax
from jax.experimental import pallas as pl
from jax.experimental.pallas import tpu as pltpu
from jax.sharding import PartitionSpec as P

BUCKETS = 4
STEP = 20
BETA_ONE = 0.8
BETA_TWO = 0.95
LEARN_RATE = 0.02
DECAY_RATE = 0.1
EPSILON = 1e-08

TOKENS = 128
FF = 27648
RANK = 32
MODEL = 5120
WIDTH = MODEL // 4
BUCKET_ROWS = FF // BUCKETS
OWNED = 108
LANES = 128
ZS, YS = 8, 4
HALF = ZS // 2
Z_STEPS = (3, 2, 1)
Z_PARTNER = 7
Y_ORDER = (0, 2, 3, 1)
BF16, F32 = jnp.bfloat16, jnp.float32
VMEM = pl.BlockSpec(memory_space=pltpu.VMEM)
ANY = pl.BlockSpec(memory_space=pl.ANY)
HBM = pl.BlockSpec(memory_space=pltpu.HBM)
CONTRACT_LAST = (((1,), (1,)), ((), ()))


def params(mib=16):
    return pltpu.CompilerParams(vmem_limit_bytes=mib * 1024 * 1024)


def in_hbm(array):
    return pltpu.with_memory_space_constraint(array, pltpu.HBM)


def shaped(shape, dtype):
    return jax.ShapeDtypeStruct(shape, dtype)


def z_pos():
    return lax.axis_index("dp") // 8


def y_pos():
    return (lax.axis_index("dp") // 2) % YS


def core_pos():
    return lax.axis_index("dp") % 2


def over_dp(value, zx=0, dy=0, dc=0):
    pairs = []
    for z in range(ZS):
        for y in range(YS):
            for c in range(2):
                target = (z ^ zx) * 8 + ((y + dy) % YS) * 2 + (c + dc) % 2
                pairs.append((z * 8 + y * 2 + c, target))
    return lax.ppermute(value, "dp", pairs)


def over_section(value, steps):
    return lax.ppermute(value, "section", [(i, (i + steps) % 4) for i in range(4)])


def slice_kernel(db_ref, ua_ref, *refs):
    outs, sems = refs[:4], refs[4]
    here, core = lax.axis_index("section"), core_pos()
    copies = []
    for k, out in enumerate(outs):
        start = lax.rem(here + k, 4) * WIDTH
        whole = pl.ds(pl.multiple_of(start, LANES), WIDTH)
        half = pl.ds(pl.multiple_of(start + core * (WIDTH // 2), LANES), WIDTH // 2)
        for i, (source, target) in enumerate(
            (
                (db_ref.at[:, whole], out.at[:, pl.ds(0, WIDTH)]),
                (ua_ref.at[:, half], out.at[:, pl.ds(WIDTH, WIDTH // 2)]),
            )
        ):
            copies.append(pltpu.make_async_copy(source, target, sems.at[2 * k + i]))
            copies[-1].start()
    for copy in copies:
        copy.wait()


def slices(db, ua):
    return pl.pallas_call(
        slice_kernel,
        out_shape=[shaped((RANK, WIDTH + WIDTH // 2), BF16)] * 4,
        in_specs=[HBM] * 2,
        out_specs=[VMEM] * 4,
        scratch_shapes=[pltpu.SemaphoreType.DMA((8,))],
        compiler_params=params(4),
        name="slices",
    )(in_hbm(db), in_hbm(ua))


def activation_kernel(slope, first, parts, pre_ref, out_ref, held, sems):
    size = held.shape[1] // parts
    copies = []
    for i in range(parts):
        copies.append(
            pltpu.make_async_copy(
                pre_ref.at[:, pl.ds(first + i * size, size)],
                held.at[:, pl.ds(i * size, size)],
                sems.at[i],
            )
        )
        copies[-1].start()

    def chunk(i, _):
        columns = pl.ds(pl.multiple_of(i * 256, 256), 256)
        for row in range(0, TOKENS, 32):
            rows = slice(row, row + 32)
            half = 0.5 * held[rows, columns].astype(F32)
            t = jnp.tanh(half)
            value = (1.0 + t) * (1.0 + half * (1.0 - t)) if slope else half + half * t
            out_ref[rows, columns] = value.astype(BF16)
        return 0

    for i, copy in enumerate(copies):
        copy.wait()
        lax.fori_loop(i * size // 256, (i + 1) * size // 256, chunk, 0)


def activation(pre, slope, bucket, count=1):
    width, parts = BUCKET_ROWS * count, 3 * count
    return pl.pallas_call(
        functools.partial(activation_kernel, slope, bucket * BUCKET_ROWS, parts),
        out_shape=shaped((TOKENS, width), BF16),
        in_specs=[HBM],
        out_specs=VMEM,
        scratch_shapes=[
            pltpu.VMEM((TOKENS, width), BF16),
            pltpu.SemaphoreType.DMA((parts,)),
        ],
        compiler_params=params(4 * count + 2),
        cost_estimate=pl.CostEstimate(
            flops=10 * TOKENS * width,
            bytes_accessed=4 * TOKENS * width,
            transcendentals=TOKENS * width,
        ),
        name="slope" if slope else "hidden",
    )(in_hbm(pre))


def share_kernel(g_ref, w0, w1, w2, w3, *outs):
    ws = (w0, w1, w2, w3)
    half = pl.ds(pl.multiple_of(core_pos() * (WIDTH // 2), LANES), WIDTH // 2)
    for k, out in enumerate(outs):
        out[:, 0:LANES] = lax.dot_general(
            ws[k][:, 0:WIDTH], g_ref[...], CONTRACT_LAST, preferred_element_type=F32
        )
        rows = jnp.concatenate([ws[(k - m) % 4][:, WIDTH:] for m in (1, 2, 3, 0)], axis=0)
        out[:, LANES:] = lax.dot_general(
            ws[k][:, half], rows, CONTRACT_LAST, preferred_element_type=F32
        )


def shares(g, ws):
    return pl.pallas_call(
        share_kernel,
        out_shape=[shaped((RANK, 2 * LANES), F32)] * 4,
        in_specs=[VMEM] * 5,
        out_specs=[VMEM] * 4,
        compiler_params=params(),
        name="shares",
    )(g, *ws)


def low_of(total, other_ref, above_ref):
    factors = total[:, LANES:] + other_ref[...]
    return total[:, 0:LANES] + jnp.dot(
        factors[:, 0 : 3 * RANK],
        above_ref[...].astype(F32),
        preferred_element_type=F32,
        precision=lax.Precision.HIGHEST,
    )


def relay_kernel(top, s0, s1, s2, s3, *refs):
    total = s0[...] + s1[...] + s2[...] + s3[...]
    if top:
        *slope_refs, da_ref, ub_ref, out_ref, part_ref = refs
        part_ref[...] = total[:, LANES:]
        low = total[:, 0:LANES]
    else:
        other_ref, above_ref, *slope_refs, da_ref, ub_ref, out_ref = refs
        low = low_of(total, other_ref, above_ref)
    low = low.T.astype(BF16)
    total = jnp.zeros((RANK, TOKENS), F32)
    start = 0
    for slope_ref in slope_refs:
        for first in range(0, slope_ref.shape[1], 768):
            columns = slice(start, start + 768)
            upstream = jnp.dot(low, da_ref[:, columns], preferred_element_type=F32)
            slope = slope_ref[:, first : first + 768].astype(F32)
            delta = (upstream * slope).astype(BF16)
            total = total + lax.dot_general(
                ub_ref[:, columns], delta, CONTRACT_LAST, preferred_element_type=F32
            )
            start += 768
    out_ref[0:RANK, :] = (0.5 * total).astype(BF16)
    if top:
        out_ref[RANK:, :] = jnp.zeros((2 * RANK, LANES), BF16)
    else:
        out_ref[RANK:, :] = above_ref[0 : 2 * RANK, :]


def relay(share, above, slope, da, ub):
    message = shaped((3 * RANK, LANES), BF16)
    top = not above
    return pl.pallas_call(
        functools.partial(relay_kernel, top),
        out_shape=[message, shaped((RANK, LANES), F32)] if top else message,
        in_specs=[VMEM] * (8 + len(above)),
        out_specs=[VMEM] * 2 if top else VMEM,
        compiler_params=params(14),
        name="relay_first" if top else "relay",
    )(*share, *above, *slope, da, ub)


def grad_kernel(s0, s1, s2, s3, other_ref, above_ref, h0, h1, h2, h3, keep_ref, send_ref, grad):
    total = s0[...] + s1[...] + s2[...] + s3[...]
    low = low_of(total, other_ref, above_ref).astype(BF16)
    core = core_pos()
    lane = lax.broadcasted_iota(jnp.int32, (RANK, LANES), 1)
    for bucket, hidden_ref in enumerate((h0, h1, h2, h3)):
        grad[...] = jnp.dot(low, hidden_ref[...], preferred_element_type=F32)
        for z in range(ZS):
            for y in range(YS):
                pair = []
                for c in range(2):
                    start = (z * 8 + y * 2 + c) * OWNED
                    base, shift = start // LANES * LANES, start % LANES
                    piece = grad[:, base : base + LANES]
                    if shift:
                        piece = pltpu.roll(piece, LANES - shift, 1)
                    if shift + OWNED > LANES:
                        more = pltpu.roll(
                            grad[:, base + LANES : base + 2 * LANES], LANES - shift, 1
                        )
                        piece = jnp.where(lane < LANES - shift, piece, more)
                    pair.append(piece)
                keep_ref[y, z, bucket] = jnp.where(core == 0, pair[0], pair[1]).astype(BF16)
                send_ref[y, z, bucket] = jnp.where(core == 0, pair[1], pair[0]).astype(BF16)


def grads(share, above, hidden):
    return pl.pallas_call(
        grad_kernel,
        out_shape=[shaped((YS, ZS, BUCKETS, RANK, LANES), BF16)] * 2,
        in_specs=[VMEM] * 10,
        out_specs=[VMEM] * 2,
        scratch_shapes=[pltpu.VMEM((RANK, BUCKET_ROWS), F32)],
        compiler_params=params(14),
        name="grads",
    )(*share, *above, *hidden)


def core_sum_kernel(keep_ref, got_ref, own_ref, up_ref, down_ref, up_held, down_held):
    here = y_pos()
    first, second = slice(0, HALF), slice(HALF, ZS)

    def block(ahead, half):
        y = lax.rem(here + ahead, YS)
        return keep_ref[y, half].astype(F32) + got_ref[y, half].astype(F32)

    own_ref[first] = block(0, first)
    own_ref[second] = block(0, second)
    up_ref[0] = block(2, first).astype(BF16)
    up_ref[1] = block(1, second).astype(BF16)
    down_ref[0] = block(2, second).astype(BF16)
    down_ref[1] = block(3, first).astype(BF16)
    up_held[...] = block(1, first)
    down_held[...] = block(3, second)


def core_sum(keep, got):
    half = (HALF, BUCKETS, RANK, LANES)
    return pl.pallas_call(
        core_sum_kernel,
        out_shape=[shaped((ZS, BUCKETS, RANK, LANES), F32)]
        + [shaped((2, *half), BF16)] * 2
        + [shaped(half, F32)] * 2,
        in_specs=[VMEM] * 2,
        out_specs=[VMEM] * 5,
        compiler_params=params(8),
        name="core_sum",
    )(keep, got)


def y_pass_kernel(up_held, from_below, down_held, from_above, up_ref, down_ref):
    up_ref[...] = (up_held[...] + from_below[0].astype(F32)).astype(BF16)
    down_ref[...] = (down_held[...] + from_above[0].astype(F32)).astype(BF16)


def y_pass(up_held, from_below, down_held, from_above):
    return pl.pallas_call(
        y_pass_kernel,
        out_shape=[shaped((HALF, BUCKETS, RANK, LANES), BF16)] * 2,
        in_specs=[VMEM] * 4,
        out_specs=[VMEM] * 2,
        compiler_params=params(4),
        name="y_pass",
    )(up_held, from_below, down_held, from_above)


def y_sum_kernel(own_ref, from_below, from_above, last_below, last_above, out_own, *outs):
    here = z_pos()
    for step, out in zip((0, *Z_STEPS), (out_own, *outs)):
        for far in range(2):
            z = here ^ (step ^ (far * Z_PARTNER))
            place = z & (HALF - 1)
            first = from_above[1, place].astype(F32) + last_below[place].astype(F32)
            second = from_below[1, place].astype(F32) + last_above[place].astype(F32)
            total = own_ref[z] + jnp.where(z < HALF, first, second)
            out[far] = total.astype(out.dtype)


def y_sum(*terms):
    block = (2, BUCKETS, RANK, LANES)
    return pl.pallas_call(
        y_sum_kernel,
        out_shape=[shaped(block, F32)] + [shaped(block, BF16)] * 3,
        in_specs=[VMEM] * 5,
        out_specs=[VMEM] * 4,
        compiler_params=params(8),
        name="y_sum",
    )(*terms)


def z_sum_kernel(own_ref, g1, g2, g3, out_ref):
    total = own_ref[...] + g1[...].astype(F32) + g2[...].astype(F32) + g3[...].astype(F32)
    out_ref[...] = total.astype(BF16)


def z_sum(own, got):
    return pl.pallas_call(
        z_sum_kernel,
        out_shape=shaped((2, BUCKETS, RANK, LANES), BF16),
        in_specs=[VMEM] * 4,
        out_specs=VMEM,
        compiler_params=params(4),
        name="z_sum",
    )(own, *got)


def adamw_kernel(mine_ref, got_ref, own_state, partner_state, weight_out, state_out):
    weight_out[...] = jnp.zeros_like(weight_out)
    for side, state in enumerate((own_state, partner_state)):
        gradient = mine_ref[side].astype(F32) + got_ref[1 - side].astype(F32)
        gradient = gradient[:, :, 0:OWNED]
        weights = state[0]
        first_new = BETA_ONE * state[1] + (1.0 - BETA_ONE) * gradient
        second_new = BETA_TWO * state[2] + (1.0 - BETA_TWO) * gradient * gradient
        first_hat = first_new / (1.0 - BETA_ONE**STEP)
        second_hat = second_new / (1.0 - BETA_TWO**STEP)
        weights_new = weights - LEARN_RATE * (
            first_hat / (jnp.sqrt(second_hat) + EPSILON) + DECAY_RATE * weights
        )
        weight_out[side, :, :, 0:OWNED] = weights_new.astype(BF16)
        if side == 0:
            state_out[0][...] = weights_new
            state_out[1][...] = first_new
            state_out[2][...] = second_new


def adamw(mine, got, state, partner_state):
    block = shaped((BUCKETS, RANK, OWNED), F32)

    def kernel(mine_ref, got_ref, state_ref, partner_ref, weight_out, *state_out):
        adamw_kernel(mine_ref, got_ref, state_ref, partner_ref, weight_out, state_out)

    return pl.pallas_call(
        kernel,
        out_shape=[shaped((2, BUCKETS, RANK, LANES), BF16)] + [block] * 3,
        in_specs=[VMEM] * 4,
        out_specs=[VMEM] * 4,
        compiler_params=params(4),
        name="adamw",
    )(mine, got, state, partner_state)


def assemble_kernel(*refs):
    arrays, (out_ref, blocks, sems) = refs[:8], refs[8:]
    core, y_here, z_here = core_pos(), y_pos(), z_pos()
    copies = []
    for side in range(2):
        for i, k in enumerate(Y_ORDER):
            copies.append(
                pltpu.make_async_copy(
                    arrays[side * YS + i],
                    blocks.at[lax.rem(core + side, 2), lax.rem(y_here + YS - k, YS)],
                    sems.at[side * YS + i],
                )
            )
            copies[-1].start()
    for copy in copies:
        copy.wait()
    lane = lax.broadcasted_iota(jnp.int32, (RANK, LANES), 1)
    places = []
    for z in range(ZS):
        apart = z_here ^ z
        places.append(jnp.where(apart < 4, 2 * apart, 2 * (apart ^ Z_PARTNER) + 1))
    for tile in range(FF // LANES):
        value = None
        first = tile * LANES // OWNED
        last = (tile * LANES + LANES - 1) // OWNED
        for piece in range(first, last + 1):
            bucket, owner = divmod(piece, 64)
            z, y, c = owner // 8, owner // 2 % YS, owner % 2
            block = blocks[c, y, places[z], bucket].astype(F32)
            start = piece * OWNED - tile * LANES
            if start % LANES:
                block = pltpu.roll(block, start % LANES, 1)
            value = block if value is None else jnp.where(lane < start, value, block)
        out_ref[:, tile * LANES : (tile + 1) * LANES] = value.astype(BF16)


def assemble(arrays):
    return pl.pallas_call(
        assemble_kernel,
        out_shape=shaped((RANK, FF), BF16),
        in_specs=[ANY] * 8,
        out_specs=VMEM,
        scratch_shapes=[
            pltpu.VMEM((2, YS, ZS, BUCKETS, RANK, LANES), BF16),
            pltpu.SemaphoreType.DMA((8,)),
        ],
        compiler_params=params(),
        name="assemble",
    )(*arrays)


def per_device(out_grad, pre_act, down_a, down_b, up_a, up_b, master, moment, second):
    da, ub = down_a[0].T, up_b[0].T
    mine = slices(down_b[0], up_a[0].T)
    ws = [mine[0]] + [over_section(mine[k], k) for k in (1, 3, 2)]
    pre = pre_act[0]
    slope = activation(pre, True, 0, 3)
    ws, slope = lax.optimization_barrier((ws, slope))
    share = shares(out_grad, [ws[0], ws[1], ws[3], ws[2]])
    pre, _ = lax.optimization_barrier((pre, share[0]))
    slope = [slope, activation(pre, True, 3)]
    share = [share[0]] + [over_section(share[k], -k) for k in (1, 3, 2)]
    state = jnp.stack([a[0].transpose(0, 2, 1) for a in (master, moment, second)])
    above, hidden = [], []
    for buckets in ((0, 1), (2, 3), ()):
        if above:
            sent = relay(share, above, slope, da, ub)
        else:
            sent, part = relay(share, above, slope, da, ub)
            above = [over_dp(part, dc=1)]
        above = [above[0], lax.ppermute(sent, "section", [(1, 0), (2, 1), (3, 2)])]
        if buckets:
            pre, _ = lax.optimization_barrier((pre, sent))
            hidden += [activation(pre, False, b) for b in buckets]
            above, state, *hidden = lax.optimization_barrier((above, state, *hidden))
    keep, send = grads(share, above, hidden)
    own, up, down, up_held, down_held = core_sum(keep, over_dp(send, dc=1))
    state, own = lax.optimization_barrier((state, own))
    partner_state = over_dp(state, zx=Z_PARTNER)
    from_below, from_above = over_dp(up, dy=1), over_dp(down, dy=-1)
    up, down = y_pass(up_held, from_below, down_held, from_above)
    last_below, last_above = over_dp(up, dy=1), over_dp(down, dy=-1)
    last_below, partner_state = lax.optimization_barrier((last_below, partner_state))
    own, *sends = y_sum(own, from_below, from_above, last_below, last_above)
    mine = z_sum(own, [over_dp(a, zx=k) for a, k in zip(sends, Z_STEPS)])
    pair, *state = adamw(mine, over_dp(mine, zx=Z_PARTNER), state, partner_state)
    column = jnp.concatenate([pair] + [over_dp(pair, zx=k) for k in Z_STEPS[::-1]])
    plane = [column] + [over_dp(column, dy=k) for k in Y_ORDER[1:]]
    rows = assemble(plane + [over_dp(a, dc=1) for a in plane])
    return (rows.T[None], *[a.transpose(0, 2, 1)[None] for a in state])


def solution(mesh):
    return jax.shard_map(
        per_device,
        mesh=mesh,
        in_specs=(
            P("dp", "section"),
            P("section", "dp", None),
            P("section", None, None),
            P("section", None, None),
            P("section", None, None),
            P("section", None, None),
            P("section", None, "dp", None),
            P("section", None, "dp", None),
            P("section", None, "dp", None),
        ),
        out_specs=(
            P("section", None, None),
            P("section", None, "dp", None),
            P("section", None, "dp", None),
            P("section", None, "dp", None),
        ),
        check_vma=False,
    )
```

```python
import functools

import jax
import jax.numpy as jnp
from jax import lax
from jax.experimental import pallas as pl
from jax.experimental.pallas import tpu as pltpu
from jax.sharding import PartitionSpec as P

BUCKETS = 4
STEP = 20
BETA_ONE = 0.8
BETA_TWO = 0.95
LEARN_RATE = 0.02
DECAY_RATE = 0.1
EPSILON = 1e-08

TOKENS = 128
FF = 27648
RANK = 32
MODEL = 5120
WIDTH = MODEL // 4
BUCKET_ROWS = FF // BUCKETS
OWNED = 108
LANES = 128
ZS, YS = 8, 4
HALF = ZS // 2
Z_STEPS = (3, 2, 1)
Z_PARTNER = 7
Y_ORDER = (0, 2, 3, 1)
BF16, F32 = jnp.bfloat16, jnp.float32
VMEM = pl.BlockSpec(memory_space=pltpu.VMEM)
ANY = pl.BlockSpec(memory_space=pl.ANY)
HBM = pl.BlockSpec(memory_space=pltpu.HBM)
CONTRACT_LAST = (((1,), (1,)), ((), ()))


def params(mib=16):
    return pltpu.CompilerParams(vmem_limit_bytes=mib * 1024 * 1024)


def in_hbm(array):
    return pltpu.with_memory_space_constraint(array, pltpu.HBM)


def shaped(shape, dtype):
    return jax.ShapeDtypeStruct(shape, dtype)


def z_pos():
    return lax.axis_index("dp") // 8


def y_pos():
    return (lax.axis_index("dp") // 2) % YS


def core_pos():
    return lax.axis_index("dp") % 2


def over_dp(value, zx=0, dy=0, dc=0):
    pairs = []
    for z in range(ZS):
        for y in range(YS):
            for c in range(2):
                target = (z ^ zx) * 8 + ((y + dy) % YS) * 2 + (c + dc) % 2
                pairs.append((z * 8 + y * 2 + c, target))
    return lax.ppermute(value, "dp", pairs)


def over_section(value, steps):
    return lax.ppermute(value, "section", [(i, (i + steps) % 4) for i in range(4)])


def slice_kernel(db_ref, ua_ref, *refs):
    outs, sems = refs[:4], refs[4]
    here, core = lax.axis_index("section"), core_pos()
    copies = []
    for k, out in enumerate(outs):
        start = lax.rem(here + k, 4) * WIDTH
        whole = pl.ds(pl.multiple_of(start, LANES), WIDTH)
        half = pl.ds(pl.multiple_of(start + core * (WIDTH // 2), LANES), WIDTH // 2)
        for i, (source, target) in enumerate(
            (
                (db_ref.at[:, whole], out.at[:, pl.ds(0, WIDTH)]),
                (ua_ref.at[:, half], out.at[:, pl.ds(WIDTH, WIDTH // 2)]),
            )
        ):
            copies.append(pltpu.make_async_copy(source, target, sems.at[2 * k + i]))
            copies[-1].start()
    for copy in copies:
        copy.wait()


def slices(db, ua):
    return pl.pallas_call(
        slice_kernel,
        out_shape=[shaped((RANK, WIDTH + WIDTH // 2), BF16)] * 4,
        in_specs=[HBM] * 2,
        out_specs=[VMEM] * 4,
        scratch_shapes=[pltpu.SemaphoreType.DMA((8,))],
        compiler_params=params(4),
        name="slices",
    )(in_hbm(db), in_hbm(ua))


def activation_kernel(slope, first, parts, pre_ref, out_ref, held, sems):
    size = held.shape[1] // parts
    copies = []
    for i in range(parts):
        copies.append(
            pltpu.make_async_copy(
                pre_ref.at[:, pl.ds(first + i * size, size)],
                held.at[:, pl.ds(i * size, size)],
                sems.at[i],
            )
        )
        copies[-1].start()

    def chunk(i, _):
        columns = pl.ds(pl.multiple_of(i * 256, 256), 256)
        for row in range(0, TOKENS, 32):
            rows = slice(row, row + 32)
            half = 0.5 * held[rows, columns].astype(F32)
            t = jnp.tanh(half)
            value = (1.0 + t) * (1.0 + half * (1.0 - t)) if slope else half + half * t
            out_ref[rows, columns] = value.astype(BF16)
        return 0

    for i, copy in enumerate(copies):
        copy.wait()
        lax.fori_loop(i * size // 256, (i + 1) * size // 256, chunk, 0)


def activation(pre, slope, bucket, count=1):
    width, parts = BUCKET_ROWS * count, 3 * count
    return pl.pallas_call(
        functools.partial(activation_kernel, slope, bucket * BUCKET_ROWS, parts),
        out_shape=shaped((TOKENS, width), BF16),
        in_specs=[HBM],
        out_specs=VMEM,
        scratch_shapes=[
            pltpu.VMEM((TOKENS, width), BF16),
            pltpu.SemaphoreType.DMA((parts,)),
        ],
        compiler_params=params(4 * count + 2),
        cost_estimate=pl.CostEstimate(
            flops=10 * TOKENS * width,
            bytes_accessed=4 * TOKENS * width,
            transcendentals=TOKENS * width,
        ),
        name="slope" if slope else "hidden",
    )(in_hbm(pre))


def share_kernel(g_ref, w0, w1, w2, w3, *outs):
    ws = (w0, w1, w2, w3)
    half = pl.ds(pl.multiple_of(core_pos() * (WIDTH // 2), LANES), WIDTH // 2)
    for k, out in enumerate(outs):
        out[:, 0:LANES] = lax.dot_general(
            ws[k][:, 0:WIDTH], g_ref[...], CONTRACT_LAST, preferred_element_type=F32
        )
        rows = jnp.concatenate([ws[(k - m) % 4][:, WIDTH:] for m in (1, 2, 3, 0)], axis=0)
        out[:, LANES:] = lax.dot_general(
            ws[k][:, half], rows, CONTRACT_LAST, preferred_element_type=F32
        )


def shares(g, ws):
    return pl.pallas_call(
        share_kernel,
        out_shape=[shaped((RANK, 2 * LANES), F32)] * 4,
        in_specs=[VMEM] * 5,
        out_specs=[VMEM] * 4,
        compiler_params=params(),
        name="shares",
    )(g, *ws)


def low_of(total, other_ref, above_ref):
    factors = total[:, LANES:] + other_ref[...]
    return total[:, 0:LANES] + jnp.dot(
        factors[:, 0 : 3 * RANK],
        above_ref[...].astype(F32),
        preferred_element_type=F32,
        precision=lax.Precision.HIGHEST,
    )


def relay_kernel(top, s0, s1, s2, s3, *refs):
    total = s0[...] + s1[...] + s2[...] + s3[...]
    if top:
        *slope_refs, da_ref, ub_ref, out_ref, part_ref = refs
        part_ref[...] = total[:, LANES:]
        low = total[:, 0:LANES]
    else:
        other_ref, above_ref, *slope_refs, da_ref, ub_ref, out_ref = refs
        low = low_of(total, other_ref, above_ref)
    low = low.T.astype(BF16)
    total = jnp.zeros((RANK, TOKENS), F32)
    start = 0
    for slope_ref in slope_refs:
        for first in range(0, slope_ref.shape[1], 768):
            columns = slice(start, start + 768)
            upstream = jnp.dot(low, da_ref[:, columns], preferred_element_type=F32)
            slope = slope_ref[:, first : first + 768].astype(F32)
            delta = (upstream * slope).astype(BF16)
            total = total + lax.dot_general(
                ub_ref[:, columns], delta, CONTRACT_LAST, preferred_element_type=F32
            )
            start += 768
    out_ref[0:RANK, :] = (0.5 * total).astype(BF16)
    if top:
        out_ref[RANK:, :] = jnp.zeros((2 * RANK, LANES), BF16)
    else:
        out_ref[RANK:, :] = above_ref[0 : 2 * RANK, :]


def relay(share, above, slope, da, ub):
    message = shaped((3 * RANK, LANES), BF16)
    top = not above
    return pl.pallas_call(
        functools.partial(relay_kernel, top),
        out_shape=[message, shaped((RANK, LANES), F32)] if top else message,
        in_specs=[VMEM] * (8 + len(above)),
        out_specs=[VMEM] * 2 if top else VMEM,
        compiler_params=params(14),
        name="relay_first" if top else "relay",
    )(*share, *above, *slope, da, ub)


def grad_kernel(s0, s1, s2, s3, other_ref, above_ref, h0, h1, h2, h3, keep_ref, send_ref, grad):
    total = s0[...] + s1[...] + s2[...] + s3[...]
    low = low_of(total, other_ref, above_ref).astype(BF16)
    core = core_pos()
    lane = lax.broadcasted_iota(jnp.int32, (RANK, LANES), 1)
    for bucket, hidden_ref in enumerate((h0, h1, h2, h3)):
        grad[...] = jnp.dot(low, hidden_ref[...], preferred_element_type=F32)
        for z in range(ZS):
            for y in range(YS):
                pair = []
                for c in range(2):
                    start = (z * 8 + y * 2 + c) * OWNED
                    base, shift = start // LANES * LANES, start % LANES
                    piece = grad[:, base : base + LANES]
                    if shift:
                        piece = pltpu.roll(piece, LANES - shift, 1)
                    if shift + OWNED > LANES:
                        more = pltpu.roll(
                            grad[:, base + LANES : base + 2 * LANES], LANES - shift, 1
                        )
                        piece = jnp.where(lane < LANES - shift, piece, more)
                    pair.append(piece)
                keep_ref[y, z, bucket] = jnp.where(core == 0, pair[0], pair[1]).astype(BF16)
                send_ref[y, z, bucket] = jnp.where(core == 0, pair[1], pair[0]).astype(BF16)


def grads(share, above, hidden):
    return pl.pallas_call(
        grad_kernel,
        out_shape=[shaped((YS, ZS, BUCKETS, RANK, LANES), BF16)] * 2,
        in_specs=[VMEM] * 10,
        out_specs=[VMEM] * 2,
        scratch_shapes=[pltpu.VMEM((RANK, BUCKET_ROWS), F32)],
        compiler_params=params(14),
        name="grads",
    )(*share, *above, *hidden)


def core_sum_kernel(keep_ref, got_ref, own_ref, up_ref, down_ref, up_held, down_held):
    here = y_pos()
    first, second = slice(0, HALF), slice(HALF, ZS)

    def block(ahead, half):
        y = lax.rem(here + ahead, YS)
        return keep_ref[y, half].astype(F32) + got_ref[y, half].astype(F32)

    own_ref[first] = block(0, first)
    own_ref[second] = block(0, second)
    up_ref[0] = block(2, first).astype(BF16)
    up_ref[1] = block(1, second).astype(BF16)
    down_ref[0] = block(2, second).astype(BF16)
    down_ref[1] = block(3, first).astype(BF16)
    up_held[...] = block(1, first)
    down_held[...] = block(3, second)


def core_sum(keep, got):
    half = (HALF, BUCKETS, RANK, LANES)
    return pl.pallas_call(
        core_sum_kernel,
        out_shape=[shaped((ZS, BUCKETS, RANK, LANES), F32)]
        + [shaped((2, *half), BF16)] * 2
        + [shaped(half, F32)] * 2,
        in_specs=[VMEM] * 2,
        out_specs=[VMEM] * 5,
        compiler_params=params(8),
        name="core_sum",
    )(keep, got)


def y_pass_kernel(up_held, from_below, down_held, from_above, up_ref, down_ref):
    up_ref[...] = (up_held[...] + from_below[0].astype(F32)).astype(BF16)
    down_ref[...] = (down_held[...] + from_above[0].astype(F32)).astype(BF16)


def y_pass(up_held, from_below, down_held, from_above):
    return pl.pallas_call(
        y_pass_kernel,
        out_shape=[shaped((HALF, BUCKETS, RANK, LANES), BF16)] * 2,
        in_specs=[VMEM] * 4,
        out_specs=[VMEM] * 2,
        compiler_params=params(4),
        name="y_pass",
    )(up_held, from_below, down_held, from_above)


def y_sum_kernel(own_ref, from_below, from_above, last_below, last_above, out_own, *outs):
    here = z_pos()
    for step, out in zip((0, *Z_STEPS), (out_own, *outs)):
        for far in range(2):
            z = here ^ (step ^ (far * Z_PARTNER))
            place = z & (HALF - 1)
            first = from_above[1, place].astype(F32) + last_below[place].astype(F32)
            second = from_below[1, place].astype(F32) + last_above[place].astype(F32)
            total = own_ref[z] + jnp.where(z < HALF, first, second)
            out[far] = total.astype(out.dtype)


def y_sum(*terms):
    block = (2, BUCKETS, RANK, LANES)
    return pl.pallas_call(
        y_sum_kernel,
        out_shape=[shaped(block, F32)] + [shaped(block, BF16)] * 3,
        in_specs=[VMEM] * 5,
        out_specs=[VMEM] * 4,
        compiler_params=params(8),
        name="y_sum",
    )(*terms)


def z_sum_kernel(own_ref, g1, g2, g3, out_ref):
    total = own_ref[...] + g1[...].astype(F32) + g2[...].astype(F32) + g3[...].astype(F32)
    out_ref[...] = total.astype(BF16)


def z_sum(own, got):
    return pl.pallas_call(
        z_sum_kernel,
        out_shape=shaped((2, BUCKETS, RANK, LANES), BF16),
        in_specs=[VMEM] * 4,
        out_specs=VMEM,
        compiler_params=params(4),
        name="z_sum",
    )(own, *got)


def adamw_kernel(mine_ref, got_ref, own_state, partner_state, weight_out, state_out):
    weight_out[...] = jnp.zeros_like(weight_out)
    for side, state in enumerate((own_state, partner_state)):
        gradient = mine_ref[side].astype(F32) + got_ref[1 - side].astype(F32)
        gradient = gradient[:, :, 0:OWNED]
        weights = state[0]
        first_new = BETA_ONE * state[1] + (1.0 - BETA_ONE) * gradient
        second_new = BETA_TWO * state[2] + (1.0 - BETA_TWO) * gradient * gradient
        first_hat = first_new / (1.0 - BETA_ONE**STEP)
        second_hat = second_new / (1.0 - BETA_TWO**STEP)
        weights_new = weights - LEARN_RATE * (
            first_hat / (jnp.sqrt(second_hat) + EPSILON) + DECAY_RATE * weights
        )
        weight_out[side, :, :, 0:OWNED] = weights_new.astype(BF16)
        if side == 0:
            state_out[0][...] = weights_new
            state_out[1][...] = first_new
            state_out[2][...] = second_new


def adamw(mine, got, state, partner_state):
    block = shaped((BUCKETS, RANK, OWNED), F32)

    def kernel(mine_ref, got_ref, state_ref, partner_ref, weight_out, *state_out):
        adamw_kernel(mine_ref, got_ref, state_ref, partner_ref, weight_out, state_out)

    return pl.pallas_call(
        kernel,
        out_shape=[shaped((2, BUCKETS, RANK, LANES), BF16)] + [block] * 3,
        in_specs=[VMEM] * 4,
        out_specs=[VMEM] * 4,
        compiler_params=params(4),
        name="adamw",
    )(mine, got, state, partner_state)


def assemble_kernel(*refs):
    arrays, (out_ref, blocks, rows, sems, out_sems) = refs[:8], refs[8:]
    core, y_here, z_here = core_pos(), y_pos(), z_pos()

    copies = []
    for side in range(2):
        for i, k in enumerate(Y_ORDER):
            copies.append(
                pltpu.make_async_copy(
                    arrays[side * YS + i],
                    blocks.at[lax.rem(core + side, 2), lax.rem(y_here + YS - k, YS)],
                    sems.at[side * YS + i],
                )
            )
            copies[-1].start()
    for copy in copies:
        copy.wait()
    lane = lax.broadcasted_iota(jnp.int32, (RANK, LANES), 1)
    places = []
    for z in range(ZS):
        apart = z_here ^ z
        places.append(jnp.where(apart < 4, 2 * apart, 2 * (apart ^ Z_PARTNER) + 1))
    copies = []
    for bucket in range(BUCKETS):
        for tile in range(BUCKET_ROWS // LANES):
            value = None
            first = tile * LANES // OWNED
            last = (tile * LANES + LANES - 1) // OWNED
            for owner in range(first, last + 1):
                z, y, c = owner // 8, owner // 2 % YS, owner % 2
                block = blocks[c, y, places[z], bucket]
                start = owner * OWNED - tile * LANES
                if start % LANES:
                    block = pltpu.roll(block, start % LANES, 1)
                value = block if value is None else jnp.where(lane < start, value, block)
            at = bucket * BUCKET_ROWS + tile * LANES
            rows[:, at : at + LANES] = value
        columns = pl.ds(bucket * BUCKET_ROWS, BUCKET_ROWS)
        copies.append(
            pltpu.make_async_copy(
                rows.at[:, columns], out_ref.at[:, columns], out_sems.at[bucket]
            )
        )
        copies[-1].start()
    for copy in copies:
        copy.wait()


def assemble(arrays):
    return pl.pallas_call(
        assemble_kernel,
        out_shape=shaped((RANK, FF), BF16),
        in_specs=[ANY] * 8,
        out_specs=ANY,
        scratch_shapes=[
            pltpu.VMEM((2, YS, ZS, BUCKETS, RANK, LANES), BF16),
            pltpu.VMEM((RANK, FF), BF16),
            pltpu.SemaphoreType.DMA((8,)),
            pltpu.SemaphoreType.DMA((BUCKETS,)),
        ],
        compiler_params=params(),
        name="assemble",
    )(*arrays)


def per_device(out_grad, pre_act, down_a, down_b, up_a, up_b, master, moment, second):
    da, ub = down_a[0].T, up_b[0].T
    mine = slices(down_b[0], up_a[0].T)
    ws = [mine[0]] + [over_section(mine[k], k) for k in (1, 3, 2)]
    pre = pre_act[0]
    slope = activation(pre, True, 0, 3)
    ws, slope = lax.optimization_barrier((ws, slope))
    share = shares(out_grad, [ws[0], ws[1], ws[3], ws[2]])
    pre, _ = lax.optimization_barrier((pre, share[0]))
    slope = [slope, activation(pre, True, 3)]
    share = [share[0]] + [over_section(share[k], -k) for k in (1, 3, 2)]
    state = jnp.stack([a[0].transpose(0, 2, 1) for a in (master, moment, second)])
    above, hidden = [], []
    for buckets in ((0, 1), (2, 3), ()):
        if above:
            sent = relay(share, above, slope, da, ub)
        else:
            sent, part = relay(share, above, slope, da, ub)
            above = [over_dp(part, dc=1)]
        above = [above[0], lax.ppermute(sent, "section", [(1, 0), (2, 1), (3, 2)])]
        if buckets:
            pre, _ = lax.optimization_barrier((pre, sent))
            hidden += [activation(pre, False, b) for b in buckets]
            above, state, *hidden = lax.optimization_barrier((above, state, *hidden))
    keep, send = grads(share, above, hidden)
    own, up, down, up_held, down_held = core_sum(keep, over_dp(send, dc=1))
    state, own = lax.optimization_barrier((state, own))
    partner_state = over_dp(state, zx=Z_PARTNER)
    from_below, from_above = over_dp(up, dy=1), over_dp(down, dy=-1)
    up, down = y_pass(up_held, from_below, down_held, from_above)
    last_below, last_above = over_dp(up, dy=1), over_dp(down, dy=-1)
    last_below, partner_state = lax.optimization_barrier((last_below, partner_state))
    own, *sends = y_sum(own, from_below, from_above, last_below, last_above)
    mine = z_sum(own, [over_dp(a, zx=k) for a, k in zip(sends, Z_STEPS)])
    pair, *state = adamw(mine, over_dp(mine, zx=Z_PARTNER), state, partner_state)
    column = jnp.concatenate([pair] + [over_dp(pair, zx=k) for k in Z_STEPS[::-1]])
    plane = [column] + [over_dp(column, dy=k) for k in Y_ORDER[1:]]
    rows = assemble(plane + [over_dp(a, dc=1) for a in plane])
    return (rows.T[None], *[a.transpose(0, 2, 1)[None] for a in state])


def solution(mesh):
    return jax.shard_map(
        per_device,
        mesh=mesh,
        in_specs=(
            P("dp", "section"),
            P("section", "dp", None),
            P("section", None, None),
            P("section", None, None),
            P("section", None, None),
            P("section", None, None),
            P("section", None, "dp", None),
            P("section", None, "dp", None),
            P("section", None, "dp", None),
        ),
        out_specs=(
            P("section", None, None),
            P("section", None, "dp", None),
            P("section", None, "dp", None),
            P("section", None, "dp", None),
        ),
        check_vma=False,
    )
```

```python
import functools

import jax
import jax.numpy as jnp
from jax import lax
from jax.experimental import pallas as pl
from jax.experimental.pallas import tpu as pltpu
from jax.sharding import PartitionSpec as P

BUCKETS = 4
STEP = 20
BETA_ONE = 0.8
BETA_TWO = 0.95
LEARN_RATE = 0.02
DECAY_RATE = 0.1
EPSILON = 1e-08

TOKENS = 128
FF = 27648
RANK = 32
MODEL = 5120
WIDTH = MODEL // 4
BUCKET_ROWS = FF // BUCKETS
OWNED = 108
LANES = 128
ZS, YS = 8, 4
HALF = ZS // 2
EARLY = 3
Z_STEPS = (3, 2, 1)
Z_PARTNER = 7
Y_ORDER = (0, 2, 3, 1)
BF16, F32 = jnp.bfloat16, jnp.float32
VMEM = pl.BlockSpec(memory_space=pltpu.VMEM)
ANY = pl.BlockSpec(memory_space=pl.ANY)
HBM = pl.BlockSpec(memory_space=pltpu.HBM)
CONTRACT_LAST = (((1,), (1,)), ((), ()))


def params(mib=16):
    return pltpu.CompilerParams(vmem_limit_bytes=mib * 1024 * 1024)


def in_hbm(array):
    return pltpu.with_memory_space_constraint(array, pltpu.HBM)


def shaped(shape, dtype):
    return jax.ShapeDtypeStruct(shape, dtype)


def z_pos():
    return lax.axis_index("dp") // 8


def y_pos():
    return (lax.axis_index("dp") // 2) % YS


def core_pos():
    return lax.axis_index("dp") % 2


def over_dp(value, zx=0, dy=0, dc=0):
    pairs = []
    for z in range(ZS):
        for y in range(YS):
            for c in range(2):
                target = (z ^ zx) * 8 + ((y + dy) % YS) * 2 + (c + dc) % 2
                pairs.append((z * 8 + y * 2 + c, target))
    return lax.ppermute(value, "dp", pairs)


def over_section(value, steps):
    return lax.ppermute(value, "section", [(i, (i + steps) % 4) for i in range(4)])


def slice_kernel(db_ref, ua_ref, *refs):
    outs, sems = refs[:4], refs[4]
    here, core = lax.axis_index("section"), core_pos()
    copies = []
    for k, out in enumerate(outs):
        start = lax.rem(here + k, 4) * WIDTH
        whole = pl.ds(pl.multiple_of(start, LANES), WIDTH)
        half = pl.ds(pl.multiple_of(start + core * (WIDTH // 2), LANES), WIDTH // 2)
        for i, (source, target) in enumerate(
            (
                (db_ref.at[:, whole], out.at[:, pl.ds(0, WIDTH)]),
                (ua_ref.at[:, half], out.at[:, pl.ds(WIDTH, WIDTH // 2)]),
            )
        ):
            copies.append(pltpu.make_async_copy(source, target, sems.at[2 * k + i]))
            copies[-1].start()
    for copy in copies:
        copy.wait()


def slices(db, ua):
    return pl.pallas_call(
        slice_kernel,
        out_shape=[shaped((RANK, WIDTH + WIDTH // 2), BF16)] * 4,
        in_specs=[HBM] * 2,
        out_specs=[VMEM] * 4,
        scratch_shapes=[pltpu.SemaphoreType.DMA((8,))],
        compiler_params=params(4),
        name="slices",
    )(in_hbm(db), in_hbm(ua))


def activation_kernel(slope, first, parts, pre_ref, out_ref, held, sems):
    size = held.shape[1] // parts
    copies = []
    for i in range(parts):
        copies.append(
            pltpu.make_async_copy(
                pre_ref.at[:, pl.ds(first + i * size, size)],
                held.at[:, pl.ds(i * size, size)],
                sems.at[i],
            )
        )
        copies[-1].start()

    def chunk(i, _):
        columns = pl.ds(pl.multiple_of(i * 256, 256), 256)
        for row in range(0, TOKENS, 32):
            rows = slice(row, row + 32)
            half = 0.5 * held[rows, columns].astype(F32)
            t = jnp.tanh(half)
            value = (1.0 + t) * (1.0 + half * (1.0 - t)) if slope else half + half * t
            out_ref[rows, columns] = value.astype(BF16)
        return 0

    for i, copy in enumerate(copies):
        copy.wait()
        lax.fori_loop(i * size // 256, (i + 1) * size // 256, chunk, 0)


def activation(pre, slope, bucket, count=1):
    width, parts = BUCKET_ROWS * count, 3 * count
    return pl.pallas_call(
        functools.partial(activation_kernel, slope, bucket * BUCKET_ROWS, parts),
        out_shape=shaped((TOKENS, width), BF16),
        in_specs=[HBM],
        out_specs=VMEM,
        scratch_shapes=[
            pltpu.VMEM((TOKENS, width), BF16),
            pltpu.SemaphoreType.DMA((parts,)),
        ],
        compiler_params=params(4 * count + 2),
        cost_estimate=pl.CostEstimate(
            flops=10 * TOKENS * width,
            bytes_accessed=4 * TOKENS * width,
            transcendentals=TOKENS * width,
        ),
        name="slope" if slope else "hidden",
    )(in_hbm(pre))


def share_kernel(g_ref, w0, w1, w2, w3, *outs):
    ws = (w0, w1, w2, w3)
    half = pl.ds(pl.multiple_of(core_pos() * (WIDTH // 2), LANES), WIDTH // 2)
    for k, out in enumerate(outs):
        out[:, 0:LANES] = lax.dot_general(
            ws[k][:, 0:WIDTH], g_ref[...], CONTRACT_LAST, preferred_element_type=F32
        )
        rows = jnp.concatenate([ws[(k - m) % 4][:, WIDTH:] for m in (1, 2, 3, 0)], axis=0)
        out[:, LANES:] = lax.dot_general(
            ws[k][:, half], rows, CONTRACT_LAST, preferred_element_type=F32
        )


def shares(g, ws):
    return pl.pallas_call(
        share_kernel,
        out_shape=[shaped((RANK, 2 * LANES), F32)] * 4,
        in_specs=[VMEM] * 5,
        out_specs=[VMEM] * 4,
        compiler_params=params(),
        name="shares",
    )(g, *ws)


def low_of(total, other_ref, above_ref):
    factors = total[:, LANES:] + other_ref[...]
    return total[:, 0:LANES] + jnp.dot(
        factors[:, 0 : 3 * RANK],
        above_ref[...].astype(F32),
        preferred_element_type=F32,
        precision=lax.Precision.HIGHEST,
    )


def relay_kernel(top, s0, s1, s2, s3, *refs):
    total = s0[...] + s1[...] + s2[...] + s3[...]
    if top:
        *slope_refs, da_ref, ub_ref, out_ref, part_ref = refs
        part_ref[...] = total[:, LANES:]
        low = total[:, 0:LANES]
    else:
        other_ref, above_ref, *slope_refs, da_ref, ub_ref, out_ref = refs
        low = low_of(total, other_ref, above_ref)
    low = low.T.astype(BF16)
    total = jnp.zeros((RANK, TOKENS), F32)
    start = 0
    for slope_ref in slope_refs:
        for first in range(0, slope_ref.shape[1], 768):
            columns = slice(start, start + 768)
            upstream = jnp.dot(low, da_ref[:, columns], preferred_element_type=F32)
            slope = slope_ref[:, first : first + 768].astype(F32)
            delta = (upstream * slope).astype(BF16)
            total = total + lax.dot_general(
                ub_ref[:, columns], delta, CONTRACT_LAST, preferred_element_type=F32
            )
            start += 768
    out_ref[0:RANK, :] = (0.5 * total).astype(BF16)
    if top:
        out_ref[RANK:, :] = jnp.zeros((2 * RANK, LANES), BF16)
    else:
        out_ref[RANK:, :] = above_ref[0 : 2 * RANK, :]


def relay(share, above, slope, da, ub):
    message = shaped((3 * RANK, LANES), BF16)
    top = not above
    return pl.pallas_call(
        functools.partial(relay_kernel, top),
        out_shape=[message, shaped((RANK, LANES), F32)] if top else message,
        in_specs=[VMEM] * (8 + len(above)),
        out_specs=[VMEM] * 2 if top else VMEM,
        compiler_params=params(14),
        name="relay_first" if top else "relay",
    )(*share, *above, *slope, da, ub)


def grad_kernel(s0, s1, s2, s3, other_ref, above_ref, h0, h1, h2, h3, keep_ref, send_ref, grad):
    total = s0[...] + s1[...] + s2[...] + s3[...]
    low = low_of(total, other_ref, above_ref).astype(BF16)
    core = core_pos()
    lane = lax.broadcasted_iota(jnp.int32, (RANK, LANES), 1)
    for bucket, hidden_ref in enumerate((h0, h1, h2, h3)):
        grad[...] = jnp.dot(low, hidden_ref[...], preferred_element_type=F32)
        for z in range(ZS):
            for y in range(YS):
                pair = []
                for c in range(2):
                    start = (z * 8 + y * 2 + c) * OWNED
                    base, shift = start // LANES * LANES, start % LANES
                    piece = grad[:, base : base + LANES]
                    if shift:
                        piece = pltpu.roll(piece, LANES - shift, 1)
                    if shift + OWNED > LANES:
                        more = pltpu.roll(
                            grad[:, base + LANES : base + 2 * LANES], LANES - shift, 1
                        )
                        piece = jnp.where(lane < LANES - shift, piece, more)
                    pair.append(piece)
                keep_ref[y, z, bucket] = jnp.where(core == 0, pair[0], pair[1]).astype(BF16)
                send_ref[y, z, bucket] = jnp.where(core == 0, pair[1], pair[0]).astype(BF16)


def grads(share, above, hidden):
    return pl.pallas_call(
        grad_kernel,
        out_shape=[shaped((YS, ZS, BUCKETS, RANK, LANES), BF16)] * 2,
        in_specs=[VMEM] * 10,
        out_specs=[VMEM] * 2,
        scratch_shapes=[pltpu.VMEM((RANK, BUCKET_ROWS), F32)],
        compiler_params=params(14),
        name="grads",
    )(*share, *above, *hidden)


def core_sum_kernel(
    keep_ref, got_ref, own_ref, up_ref, down_ref, up_held, down_held, up_late, down_late
):
    here = y_pos()
    first, second = slice(0, HALF), slice(HALF, ZS)
    direct = slice(HALF, HALF + EARLY)

    def block(ahead, half):
        y = lax.rem(here + ahead, YS)
        return keep_ref[y, half].astype(F32) + got_ref[y, half].astype(F32)

    own_ref[first] = block(0, first)
    own_ref[second] = block(0, second)
    up_ref[first] = block(2, first).astype(BF16)
    up_ref[direct] = block(1, slice(HALF, HALF + EARLY)).astype(BF16)
    up_late[...] = block(1, slice(HALF + EARLY, ZS)).astype(BF16)
    down_ref[first] = block(2, second).astype(BF16)
    down_ref[direct] = block(3, slice(0, EARLY)).astype(BF16)
    down_late[...] = block(3, slice(EARLY, HALF)).astype(BF16)
    up_held[...] = block(1, first)
    down_held[...] = block(3, second)


def core_sum(keep, got):
    half = (HALF, BUCKETS, RANK, LANES)
    return pl.pallas_call(
        core_sum_kernel,
        out_shape=[shaped((ZS, BUCKETS, RANK, LANES), F32)]
        + [shaped((HALF + EARLY, *half[1:]), BF16)] * 2
        + [shaped(half, F32)] * 2
        + [shaped((HALF - EARLY, *half[1:]), BF16)] * 2,
        in_specs=[VMEM] * 2,
        out_specs=[VMEM] * 7,
        compiler_params=params(8),
        name="core_sum",
    )(keep, got)


def y_pass_kernel(
    up_held, up_late, from_below, down_held, down_late, from_above, up_ref, down_ref
):
    for out, held, late, got in (
        (up_ref, up_held, up_late, from_below),
        (down_ref, down_held, down_late, from_above),
    ):
        out[0:HALF] = (held[...] + got[0:HALF].astype(F32)).astype(BF16)
        out[HALF:] = late[...]


def y_pass(*terms):
    return pl.pallas_call(
        y_pass_kernel,
        out_shape=[shaped((ZS - EARLY, BUCKETS, RANK, LANES), BF16)] * 2,
        in_specs=[VMEM] * 6,
        out_specs=[VMEM] * 2,
        compiler_params=params(4),
        name="y_pass",
    )(*terms)


def y_sum_kernel(own_ref, from_below, from_above, last_below, last_above, out_own, *outs):
    here = z_pos()
    for step, out in zip((0, *Z_STEPS), (out_own, *outs)):
        for far in range(2):
            z = here ^ (step ^ (far * Z_PARTNER))
            place = z & (HALF - 1)
            early = HALF + jnp.minimum(place, EARLY - 1)
            late = HALF + jnp.maximum(place - EARLY, 0)
            above = jnp.where(place < EARLY, from_above[early], last_above[late])
            below = jnp.where(place < EARLY, from_below[early], last_below[late])
            first = above.astype(F32) + last_below[place].astype(F32)
            second = below.astype(F32) + last_above[place].astype(F32)
            total = own_ref[z] + jnp.where(z < HALF, first, second)
            out[far] = total.astype(out.dtype)


def y_sum(*terms):
    block = (2, BUCKETS, RANK, LANES)
    return pl.pallas_call(
        y_sum_kernel,
        out_shape=[shaped(block, F32)] + [shaped(block, BF16)] * 3,
        in_specs=[VMEM] * 5,
        out_specs=[VMEM] * 4,
        compiler_params=params(8),
        name="y_sum",
    )(*terms)


def z_sum_kernel(own_ref, g1, g2, g3, out_ref):
    total = own_ref[...] + g1[...].astype(F32) + g2[...].astype(F32) + g3[...].astype(F32)
    out_ref[...] = total.astype(BF16)


def z_sum(own, got):
    return pl.pallas_call(
        z_sum_kernel,
        out_shape=shaped((2, BUCKETS, RANK, LANES), BF16),
        in_specs=[VMEM] * 4,
        out_specs=VMEM,
        compiler_params=params(4),
        name="z_sum",
    )(own, *got)


def adamw_kernel(mine_ref, got_ref, own_state, partner_state, weight_out, state_out):
    weight_out[...] = jnp.zeros_like(weight_out)
    for side, state in enumerate((own_state, partner_state)):
        gradient = mine_ref[side].astype(F32) + got_ref[1 - side].astype(F32)
        gradient = gradient[:, :, 0:OWNED]
        weights = state[0]
        first_new = BETA_ONE * state[1] + (1.0 - BETA_ONE) * gradient
        second_new = BETA_TWO * state[2] + (1.0 - BETA_TWO) * gradient * gradient
        first_hat = first_new / (1.0 - BETA_ONE**STEP)
        second_hat = second_new / (1.0 - BETA_TWO**STEP)
        weights_new = weights - LEARN_RATE * (
            first_hat / (jnp.sqrt(second_hat) + EPSILON) + DECAY_RATE * weights
        )
        weight_out[side, :, :, 0:OWNED] = weights_new.astype(BF16)
        if side == 0:
            state_out[0][...] = weights_new
            state_out[1][...] = first_new
            state_out[2][...] = second_new


def adamw(mine, got, state, partner_state):
    block = shaped((BUCKETS, RANK, OWNED), F32)

    def kernel(mine_ref, got_ref, state_ref, partner_ref, weight_out, *state_out):
        adamw_kernel(mine_ref, got_ref, state_ref, partner_ref, weight_out, state_out)

    return pl.pallas_call(
        kernel,
        out_shape=[shaped((2, BUCKETS, RANK, LANES), BF16)] + [block] * 3,
        in_specs=[VMEM] * 4,
        out_specs=[VMEM] * 4,
        compiler_params=params(4),
        name="adamw",
    )(mine, got, state, partner_state)


def assemble_kernel(*refs):
    arrays, (out_ref, blocks, rows, sems, out_sems) = refs[:8], refs[8:]
    core, y_here, z_here = core_pos(), y_pos(), z_pos()

    copies = []
    for side in range(2):
        for i, k in enumerate(Y_ORDER):
            copies.append(
                pltpu.make_async_copy(
                    arrays[side * YS + i],
                    blocks.at[lax.rem(core + side, 2), lax.rem(y_here + YS - k, YS)],
                    sems.at[side * YS + i],
                )
            )
            copies[-1].start()
    for copy in copies:
        copy.wait()
    lane = lax.broadcasted_iota(jnp.int32, (RANK, LANES), 1)
    places = []
    for z in range(ZS):
        apart = z_here ^ z
        places.append(jnp.where(apart < 4, 2 * apart, 2 * (apart ^ Z_PARTNER) + 1))
    copies = []
    for bucket in range(BUCKETS):
        for tile in range(BUCKET_ROWS // LANES):
            value = None
            first = tile * LANES // OWNED
            last = (tile * LANES + LANES - 1) // OWNED
            for owner in range(first, last + 1):
                z, y, c = owner // 8, owner // 2 % YS, owner % 2
                block = blocks[c, y, places[z], bucket]
                start = owner * OWNED - tile * LANES
                if start % LANES:
                    block = pltpu.roll(block, start % LANES, 1)
                value = block if value is None else jnp.where(lane < start, value, block)
            at = bucket * BUCKET_ROWS + tile * LANES
            rows[:, at : at + LANES] = value
        columns = pl.ds(bucket * BUCKET_ROWS, BUCKET_ROWS)
        copies.append(
            pltpu.make_async_copy(
                rows.at[:, columns], out_ref.at[:, columns], out_sems.at[bucket]
            )
        )
        copies[-1].start()
    for copy in copies:
        copy.wait()


def assemble(arrays):
    return pl.pallas_call(
        assemble_kernel,
        out_shape=shaped((RANK, FF), BF16),
        in_specs=[ANY] * 8,
        out_specs=ANY,
        scratch_shapes=[
            pltpu.VMEM((2, YS, ZS, BUCKETS, RANK, LANES), BF16),
            pltpu.VMEM((RANK, FF), BF16),
            pltpu.SemaphoreType.DMA((8,)),
            pltpu.SemaphoreType.DMA((BUCKETS,)),
        ],
        compiler_params=params(),
        name="assemble",
    )(*arrays)


def per_device(out_grad, pre_act, down_a, down_b, up_a, up_b, master, moment, second):
    da, ub = down_a[0].T, up_b[0].T
    mine = slices(down_b[0], up_a[0].T)
    ws = [mine[0]] + [over_section(mine[k], k) for k in (1, 3, 2)]
    pre = pre_act[0]
    slope = activation(pre, True, 0, 3)
    ws, slope = lax.optimization_barrier((ws, slope))
    share = shares(out_grad, [ws[0], ws[1], ws[3], ws[2]])
    pre, _ = lax.optimization_barrier((pre, share[0]))
    slope = [slope, activation(pre, True, 3)]
    share = [share[0]] + [over_section(share[k], -k) for k in (1, 3, 2)]
    state = jnp.stack([a[0].transpose(0, 2, 1) for a in (master, moment, second)])
    above, hidden = [], []
    for buckets in ((0, 1), (2, 3), ()):
        if above:
            sent = relay(share, above, slope, da, ub)
        else:
            sent, part = relay(share, above, slope, da, ub)
            above = [over_dp(part, dc=1)]
        above = [above[0], lax.ppermute(sent, "section", [(1, 0), (2, 1), (3, 2)])]
        if buckets:
            pre, _ = lax.optimization_barrier((pre, sent))
            hidden += [activation(pre, False, b) for b in buckets]
            above, state, *hidden = lax.optimization_barrier((above, state, *hidden))
    keep, send = grads(share, above, hidden)
    own, up, down, up_held, down_held, up_late, down_late = core_sum(
        keep, over_dp(send, dc=1)
    )
    state, own = lax.optimization_barrier((state, own))
    partner_state = over_dp(state, zx=Z_PARTNER)
    from_below, from_above = over_dp(up, dy=1), over_dp(down, dy=-1)
    up, down = y_pass(up_held, up_late, from_below, down_held, down_late, from_above)
    last_below, last_above = over_dp(up, dy=1), over_dp(down, dy=-1)
    last_below, partner_state = lax.optimization_barrier((last_below, partner_state))
    own, *sends = y_sum(own, from_below, from_above, last_below, last_above)
    mine = z_sum(own, [over_dp(a, zx=k) for a, k in zip(sends, Z_STEPS)])
    pair, *state = adamw(mine, over_dp(mine, zx=Z_PARTNER), state, partner_state)
    column = jnp.concatenate([pair] + [over_dp(pair, zx=k) for k in Z_STEPS[::-1]])
    plane = [column] + [over_dp(column, dy=k) for k in Y_ORDER[1:]]
    rows = assemble(plane + [over_dp(a, dc=1) for a in plane])
    return (rows.T[None], *[a.transpose(0, 2, 1)[None] for a in state])


def solution(mesh):
    return jax.shard_map(
        per_device,
        mesh=mesh,
        in_specs=(
            P("dp", "section"),
            P("section", "dp", None),
            P("section", None, None),
            P("section", None, None),
            P("section", None, None),
            P("section", None, None),
            P("section", None, "dp", None),
            P("section", None, "dp", None),
            P("section", None, "dp", None),
        ),
        out_specs=(
            P("section", None, None),
            P("section", None, "dp", None),
            P("section", None, "dp", None),
            P("section", None, "dp", None),
        ),
        check_vma=False,
    )
```
